512 devices in a mesh: fib: 16 (over y, x), blk: 32 (over z, core).
Axes of the slice: x: 4, y: 4, z: 16, core: 2. Of those that a mesh axis runs over, the one named last changes fastest.
Arguments:
- field_data: float32 [33, 64, 512, 256], P(None, 'blk', 'fib'), may hold values from -120 to 120
- start_block: float32 [512, 64], replicated, may hold values from -6 to 6
Outputs:
- core_out: float32 [33, 64, 64, 256], P(None, 'blk', 'fib')
The draws below stay inside these ranges and needn't reach their ends.
All inputs are finite; a program needn't handle non-finite values.
Results may differ from the reference program's by a relative error of at most 0.00013.
Values sent between devices are 32-bit elements; how exact they have to be, the bound alone decides.
A program may use at most 192 MiB of HBM per device.

```python
import jax
import jax.numpy as jnp
from jax import lax

S = 33
NX = 512
RANK = 64
NY = 256
NZ = 64


def draw_field_data(key, part):
    key_base = jax.random.fold_in(key, 11)
    key_species = jax.random.fold_in(key, 12)
    key_column = jax.random.fold_in(key, 13)
    key_plane = jax.random.fold_in(key, 14)
    shape_full = (S, NZ, NX, NY)
    base_values = jnp.clip(jax.random.normal(key_base, shape_full, jnp.float32), -5.0, 5.0)
    species_scale = jnp.exp(jax.random.uniform(key_species, (S, 1, 1, 1), jnp.float32, jnp.log(0.3), jnp.log(3.0)))
    column_scale = jnp.exp(jax.random.uniform(key_column, (1, 1, NX, 1), jnp.float32, 0.0, jnp.log(4.0)))
    plane_scale = jnp.exp(jax.random.uniform(key_plane, (1, NZ, 1, 1), jnp.float32, jnp.log(0.5), jnp.log(2.0)))
    return (base_values * species_scale * column_scale * plane_scale).astype(jnp.float32)


def noise(stream_key, shape, spread, limit, held_as=jnp.bfloat16):
    return jnp.clip(spread * jax.random.normal(stream_key, shape, jnp.float32), -limit, limit).astype(held_as)


def setup_inputs(seed: int = 0) -> dict:
    splits = jax.random.split(jax.random.key(seed), 3)
    field_data = draw_field_data(jax.random.fold_in(splits[2], 71), 0)
    start_block = noise(splits[1], (NX, RANK), 1.0, 6.0, jnp.float32)
    return {"field_data": field_data, "start_block": start_block}


def reference(field_data, start_block):
    highest = lax.Precision.HIGHEST

    def accumulate(running, slab_part):
        return (running + jnp.einsum('zxy,zwy->xw', slab_part, slab_part, precision=highest), None)
    gram_total, _ = lax.scan(accumulate, jnp.zeros((NX, NX), jnp.float32), field_data)
    raw_basis = jnp.dot(gram_total, start_block, precision=highest)
    inner_block = jnp.dot(raw_basis.T, raw_basis, precision=highest)
    lower_factor = jnp.linalg.cholesky(inner_block)
    basis_cols = jax.scipy.linalg.solve_triangular(lower_factor, raw_basis.T, lower=True).T
    core_out = jnp.einsum('szxy,xr->szry', field_data, basis_cols, precision=highest)
    return core_out
```

```python
import functools

import jax
import jax.numpy as jnp
from jax import lax
from jax.experimental import pallas as pl
from jax.experimental.pallas import tpu as pltpu
from jax.sharding import PartitionSpec as P

MESH = pl.DeviceIdType.MESH
HIGHEST = lax.Precision.HIGHEST
CORES = 2
NT = (((1,), (1,)), ((), ()))


def owner_of(unit, shift, side):
    if side == 4:
        return unit * 4 + lax.rem(unit + shift, 4)
    return unit


def eliminate(inner, rank):
    wide = inner.shape[1]
    rows = lax.broadcasted_iota(jnp.int32, (rank, wide), 0)
    lanes = lax.broadcasted_iota(jnp.int32, (rank, wide), 1)
    augmented = jnp.where(lanes == rows + rank, 1.0, inner)
    blocks = [augmented[8 * i : 8 * i + 8, :] for i in range(rank // 8)]
    sub = lax.broadcasted_iota(jnp.int32, (8, 1), 0)
    for k in range(rank):
        kb, kr = divmod(k, 8)
        pivot_row = blocks[kb][kr : kr + 1, :]
        scaled = pivot_row * (1.0 / pivot_row[:, k : k + 1])
        for i in range(kb, rank // 8):
            column = blocks[i][:, k : k + 1]
            if i == kb:
                column = jnp.where(sub > kr, column, 0.0)
            blocks[i] = blocks[i] - column * scaled
    reduced = jnp.concatenate(blocks, axis=0)
    pivots = jnp.sum(jnp.where(lanes == rows, reduced, 0.0), axis=1, keepdims=True)
    return reduced * (1.0 / jnp.sqrt(pivots))


def kernel(nf, nz, field, start, out, fbuf, lbuf, part, rbuf, zsrc, zbuf, gsrc, gbuf, osrc, lsrc,
           a_send, a_recv, own_sem, l_send, l_recv, r_send, r_recv, z_send, z_recv, g_send, g_recv,
           o_send, o_recv, p_send, p_recv, own_out):
    side = {16: 4, 4: 2}[nf]
    width_x = field.shape[2]
    rank = start.shape[1]
    last = field.shape[0] - 1
    plane = nf * CORES
    f = lax.axis_index("fib")
    b = lax.axis_index("blk")
    core, z = lax.rem(b, CORES), lax.div(b, CORES)
    t = f * CORES + core
    row, col = lax.div(f, side), lax.rem(f, side)
    shift = lax.rem(b, 4)

    def plane_peer(k):
        other = lax.rem(t + k, plane)
        return other, {"fib": lax.div(other, CORES), "blk": z * CORES + lax.rem(other, CORES)}

    def z_peer(k):
        return {"fib": f, "blk": lax.rem(z + k, nz) * CORES + core}

    def fib_peer(k):
        return lax.rem(row + lax.div(k, side), side) * side + lax.rem(col + lax.rem(k, side), side)

    barrier = pltpu.get_barrier_semaphore()

    def greet_plane(k, _):
        pl.semaphore_signal(barrier, inc=1, device_id=plane_peer(k)[1], device_id_type=MESH)
        return 0

    def greet_z(k, _):
        pl.semaphore_signal(barrier, inc=1, device_id=z_peer(k), device_id_type=MESH)
        return 0

    lax.fori_loop(1, plane, greet_plane, 0)
    lax.fori_loop(1, nz, greet_z, 0)
    own = pltpu.make_async_copy(
        field.at[pl.ds(2 * f, 2)], fbuf.at[:, :, pl.ds(pl.multiple_of(f * width_x, width_x), width_x), :], own_sem)
    own.start()
    pl.semaphore_wait(barrier, plane - 1 + nz - 1)

    mine = pl.ds(pl.multiple_of(f * width_x, width_x), width_x)
    for u in range(4):
        owner = owner_of(u, shift, side)
        source = field.at[last, u // 2, :, pl.ds((u % 2) * 128, 128)]

        @pl.when(owner != f)
        def _():
            pltpu.make_async_remote_copy(source, lbuf.at[mine, :], l_send, l_recv, {"fib": owner, "blk": b}, MESH).start()

        @pl.when(owner == f)
        def _():
            pltpu.make_async_copy(source, lbuf.at[mine, :], own_out).start()

    for q in range(4):
        def send_pair(k, _, q=q):
            peer = fib_peer(k)
            pltpu.make_async_remote_copy(
                field.at[2 * peer + q // 2, q % 2], fbuf.at[q // 2, q % 2, mine, :], a_send, a_recv.at[q],
                {"fib": peer, "blk": b}, MESH).start()
            return 0

        lax.fori_loop(1, nf, send_pair, 0)

    others = pl.ds(0, (nf - 1) * width_x)
    start_t = jnp.transpose(start[...])
    own.wait()
    raw = jnp.zeros((start.shape[0], rank), jnp.float32)
    for q in range(4):
        whole = fbuf.at[q // 2, q % 2]
        pltpu.make_async_copy(whole.at[others, :], whole.at[others, :], a_recv.at[q]).wait()
        fibres = whole[...]
        projected = jnp.dot(start_t, fibres, precision=HIGHEST, preferred_element_type=jnp.float32)
        raw = raw + lax.dot_general(fibres, projected, NT, precision=HIGHEST, preferred_element_type=jnp.float32)
    raw_t = jnp.transpose(raw)
    tiles_x = start.shape[0] // 128
    for i in range(rank // 8):
        for j in range(tiles_x):
            part[i * tiles_x + j] = raw_t[8 * i : 8 * i + 8, 128 * j : 128 * j + 128]

    row_unit = row if side == 4 else f
    is_owner = owner_of(row_unit, shift, side) == f

    @pl.when(is_owner)
    def _():
        pltpu.make_async_copy(lbuf.at[others, :], lbuf.at[others, :], l_recv).wait()
        pltpu.make_async_copy(lbuf.at[mine, :], lbuf.at[mine, :], own_out).wait()
        fibres = lbuf[...]
        projected = jnp.dot(start_t, fibres, precision=HIGHEST, preferred_element_type=jnp.float32)
        extra = jnp.transpose(
            lax.dot_general(fibres, projected, NT, precision=HIGHEST, preferred_element_type=jnp.float32))
        for i in range(rank // 8):
            for j in range(tiles_x):
                part[i * tiles_x + j] += extra[8 * i : 8 * i + 8, 128 * j : 128 * j + 128]

    def scatter(k, _):
        other, device = plane_peer(k)
        pltpu.make_async_remote_copy(part.at[other], rbuf.at[t], r_send, r_recv, device, MESH).start()
        return 0

    lax.fori_loop(1, plane, scatter, 0)
    rbuf[t] = part[t]
    rest = pl.ds(0, plane - 1)
    pltpu.make_async_copy(rbuf.at[rest], rbuf.at[rest], r_recv).wait()
    tile = jnp.sum(rbuf[...], axis=0)
    zsrc[...] = tile
    zbuf[z] = tile

    def exchange(k, _):
        pltpu.make_async_remote_copy(zsrc, zbuf.at[z], z_send, z_recv, z_peer(k), MESH).start()
        return 0

    lax.fori_loop(1, nz, exchange, 0)
    rest_z = pl.ds(0, nz - 1)
    pltpu.make_async_copy(zbuf.at[rest_z], zbuf.at[rest_z], z_recv).wait()
    tile = jnp.sum(zbuf[...], axis=0)
    gsrc[...] = tile
    gbuf[t] = tile

    def gather(k, _):
        pltpu.make_async_remote_copy(gsrc, gbuf.at[t], g_send, g_recv, plane_peer(k)[1], MESH).start()
        return 0

    lax.fori_loop(1, plane, gather, 0)
    pltpu.make_async_copy(gbuf.at[rest], gbuf.at[rest], g_recv).wait()
    total_t = jnp.concatenate(
        [jnp.concatenate([gbuf[i * tiles_x + j] for j in range(tiles_x)], axis=1) for i in range(rank // 8)], axis=0)

    padding = jnp.zeros((128 - rank, total_t.shape[1]), jnp.float32)
    inner = lax.dot_general(total_t, jnp.concatenate([total_t, padding], axis=0), NT, precision=HIGHEST,
                            preferred_element_type=jnp.float32)
    inverse = eliminate(inner, rank)
    pieces = [jnp.zeros((rank, total_t.shape[1]), jnp.float32), total_t]
    if 128 - 2 * rank:
        pieces.append(jnp.zeros((128 - 2 * rank, total_t.shape[1]), jnp.float32))
    basis_t = jnp.dot(inverse, jnp.concatenate(pieces, axis=0), precision=HIGHEST, preferred_element_type=jnp.float32)

    share = rank // nf
    for s in range(2):
        for zz in range(2):
            core_part = jnp.dot(basis_t, fbuf[s, zz], precision=HIGHEST, preferred_element_type=jnp.float32)
            for j in range(nf):
                osrc[j, s, zz] = core_part[share * j : share * j + share, :]

        def send_core(k, _, s=s):
            peer = fib_peer(k)
            pltpu.make_async_remote_copy(osrc.at[peer, s], out.at[2 * f + s], o_send, o_recv,
                                         {"fib": peer, "blk": b}, MESH).start()
            return 0

        lax.fori_loop(1, nf, send_core, 0)
    own_core = pltpu.make_async_copy(osrc.at[f], out.at[pl.ds(2 * f, 2)], own_sem)
    own_core.start()

    @pl.when(is_owner)
    def _():
        core_part = jnp.dot(basis_t, lbuf[...], precision=HIGHEST, preferred_element_type=jnp.float32)
        for j in range(nf):
            lsrc[j] = core_part[share * j : share * j + share, :]
        lanes = pl.ds(pl.multiple_of(lax.rem(row_unit, 2) * 128, 128), 128)
        target = out.at[last, lax.div(row_unit, 2), :, lanes]

        def send_last(k, _):
            peer = fib_peer(k)
            pltpu.make_async_remote_copy(lsrc.at[peer], target, p_send, p_recv, {"fib": peer, "blk": b}, MESH).start()
            return 0

        lax.fori_loop(1, nf, send_last, 0)
        own_last = pltpu.make_async_copy(lsrc.at[f], target, own_out)
        own_last.start()
        own_last.wait()

    own_core.wait()
    arrived = out.at[pl.ds(0, 2 * (nf - 1))]
    pltpu.make_async_copy(arrived, arrived, o_recv).wait()
    pltpu.make_async_copy(arrived, arrived, o_send).wait()
    sent = fbuf.at[:, :, others, :]
    pltpu.make_async_copy(sent, sent, a_send).wait()
    pltpu.make_async_copy(rbuf.at[rest], rbuf.at[rest], r_send).wait()
    pltpu.make_async_copy(zbuf.at[rest_z], zbuf.at[rest_z], z_send).wait()
    pltpu.make_async_copy(gbuf.at[rest], gbuf.at[rest], g_send).wait()

    def finish_last(owned):
        units = 4 - owned
        pltpu.make_async_copy(lsrc.at[pl.ds(0, units)], lsrc.at[pl.ds(0, units)], p_recv).wait()
        slab = lbuf.at[pl.ds(0, units * width_x), :]
        pltpu.make_async_copy(slab, slab, l_send).wait()

    @pl.when(is_owner)
    def _():
        finish_last(1)
        pltpu.make_async_copy(lsrc.at[pl.ds(0, nf - 1)], lsrc.at[pl.ds(0, nf - 1)], p_send).wait()

    if side == 4:
        @pl.when(jnp.logical_not(is_owner))
        def _():
            finish_last(0)


def solution(mesh):
    nf, nb = mesh.shape["fib"], mesh.shape["blk"]
    nz = nb // CORES

    def shards(field_data, start_block):
        species, planes, width_x, width_y = field_data.shape
        full_x, rank = start_block.shape
        share = rank // nf
        tiles = rank * full_x // 1024
        assert species == 2 * nf + 1 and planes == 2 and width_y == 256 and tiles == nf * CORES and 2 * rank <= 128
        f32 = jnp.float32
        dma = pltpu.SemaphoreType.DMA
        return pl.pallas_call(
            functools.partial(kernel, nf, nz),
            out_shape=jax.ShapeDtypeStruct((species, planes, share, width_y), f32),
            in_specs=[pl.BlockSpec(memory_space=pl.ANY), pl.BlockSpec(memory_space=pltpu.VMEM)],
            out_specs=pl.BlockSpec(memory_space=pl.ANY),
            scratch_shapes=[
                pltpu.VMEM((2, 2, full_x, width_y), f32),
                pltpu.VMEM((full_x, 128), f32),
                pltpu.VMEM((tiles, 8, 128), f32),
                pltpu.VMEM((tiles, 8, 128), f32),
                pltpu.VMEM((8, 128), f32),
                pltpu.VMEM((nz, 8, 128), f32),
                pltpu.VMEM((8, 128), f32),
                pltpu.VMEM((tiles, 8, 128), f32),
                pltpu.VMEM((nf, 2, 2, share, width_y), f32),
                pltpu.VMEM((nf, share, 128), f32),
                dma, dma((4,)), dma, dma, dma, dma, dma, dma, dma, dma, dma, dma, dma, dma, dma, dma,
            ],
            compiler_params=pltpu.CompilerParams(collective_id=0, has_side_effects=True, vmem_limit_bytes=48 << 20),
            cost_estimate=pl.CostEstimate(flops=2_000_000_000, bytes_accessed=5_000_000, transcendentals=64),
            name="hosvd_step",
        )(field_data, start_block)

    in_specs = (P(None, "blk", "fib", None), P())
    out_specs = P(None, "blk", "fib", None)
    return jax.shard_map(shards, mesh=mesh, in_specs=in_specs, out_specs=out_specs, check_vma=False)
```

```python
import functools

import jax
import jax.numpy as jnp
from jax import lax
from jax.experimental import pallas as pl
from jax.experimental.pallas import tpu as pltpu
from jax.sharding import PartitionSpec as P

MESH = pl.DeviceIdType.MESH
HIGHEST = lax.Precision.HIGHEST
CORES = 2
NT = (((1,), (1,)), ((), ()))


def owner_of(unit, shift, side):
    if side == 4:
        return unit * 4 + lax.rem(unit + shift, 4)
    return unit


def ring_distance(step, size):
    return min(step % size, -step % size)


def eliminate(inner, rank):
    wide = inner.shape[1]
    rows = lax.broadcasted_iota(jnp.int32, (rank, wide), 0)
    lanes = lax.broadcasted_iota(jnp.int32, (rank, wide), 1)
    augmented = jnp.where(lanes == rows + rank, 1.0, inner)
    blocks = [augmented[8 * i : 8 * i + 8, :] for i in range(rank // 8)]
    sub = lax.broadcasted_iota(jnp.int32, (8, wide), 0)

    def columns(block, p):
        return [jnp.broadcast_to(block[:, 8 * p + m : 8 * p + m + 1], (8, wide)) for m in range(8)]

    for p in range(rank // 8):
        panel, block = columns(blocks[p], p), blocks[p]
        pivot_rows, factors = [], []
        for j in range(8):
            inv = 1.0 / panel[j][j : j + 1, :]
            pivot_rows.append(block[j : j + 1, :] * inv)
            factors.append([panel[m][j : j + 1, :] * inv for m in range(j + 1, 8)])
            below = jnp.where(sub > j, panel[j], 0.0)
            block = block - below * pivot_rows[j]
            for m in range(j + 1, 8):
                panel[m] = panel[m] - below * factors[j][m - j - 1]
        blocks[p] = block
        for i in range(p + 1, rank // 8):
            panel, block = columns(blocks[i], p), blocks[i]
            for j in range(8):
                block = block - panel[j] * pivot_rows[j]
                for m in range(j + 1, 8):
                    panel[m] = panel[m] - panel[j] * factors[j][m - j - 1]
            blocks[i] = block
    reduced = jnp.concatenate(blocks, axis=0)
    pivots = jnp.sum(jnp.where(lanes == rows, reduced, 0.0), axis=1, keepdims=True)
    return reduced * (1.0 / jnp.sqrt(pivots))


def halves(value):
    high = value.astype(jnp.bfloat16)
    return high, (value - high.astype(jnp.float32)).astype(jnp.bfloat16)


def kernel(nf, nz, field, start_hbm, out, start_t, fbuf, lbuf, fhigh, flow, lhigh, llow, part, extra, rbuf, zsrc, zbuf,
           gsrc, gbuf, osrc, lsrc, a_send, a_recv, own_sem, start_sem, l_send, l_recv, own_last, r_send, r_recv, z_send,
           z_recv, g_send, g_recv, o_send, o_recv, p_send, p_recv):
    side = {16: 4, 4: 2}[nf]
    width_x = field.shape[2]
    rank, full_x = start_t.shape
    last = field.shape[0] - 1
    plane = nf * CORES
    f = lax.axis_index("fib")
    b = lax.axis_index("blk")
    core, z = lax.rem(b, CORES), lax.div(b, CORES)
    t = f * CORES + core
    row, col = lax.div(f, side), lax.rem(f, side)
    shift = lax.rem(b, 4)
    row_unit = row if side == 4 else f
    is_owner = owner_of(row_unit, shift, side) == f
    mine = pl.ds(pl.multiple_of(f * width_x, width_x), width_x)
    others = pl.ds(0, (nf - 1) * width_x)

    own = pltpu.make_async_copy(field.at[pl.ds(2 * f, 2)], fbuf.at[:, :, mine, :], own_sem)
    own.start()
    start_copy = pltpu.make_async_copy(start_hbm, start_t, start_sem)
    start_copy.start()

    steps = [(dy, dx) for dy in range(side) for dx in range(side)]
    steps.sort(key=lambda s: -ring_distance(s[0], side) - ring_distance(s[1], side))
    row_at = [lax.rem(row + d, side) * side for d in range(side)]
    col_at = [lax.rem(col + d, side) for d in range(side)]
    fibs = [row_at[dy] + col_at[dx] for dy, dx in steps]
    fib_peers = fibs[:-1]
    twin = z * CORES + 1 - core
    plane_peers = []
    for other in fibs:
        if other is not fibs[-1]:
            plane_peers.append((other * CORES + core, {"fib": other, "blk": b}))
        plane_peers.append((other * CORES + 1 - core, {"fib": other, "blk": twin}))
    z_steps = sorted(range(1, nz), key=lambda k: -ring_distance(k, nz))
    z_peers = [{"fib": f, "blk": lax.rem(z + k, nz) * CORES + core} for k in z_steps]

    barrier = pltpu.get_barrier_semaphore()
    for other in fib_peers:
        pl.semaphore_signal(barrier, inc=1, device_id={"fib": other, "blk": b}, device_id_type=MESH)
    for device in z_peers:
        pl.semaphore_signal(barrier, inc=1, device_id=device, device_id_type=MESH)
    for other in fibs:
        pl.semaphore_signal(barrier, inc=1, device_id={"fib": other, "blk": twin}, device_id_type=MESH)
    pl.semaphore_wait(barrier, plane - 1 + nz - 1)

    for u in range(4):
        owner = owner_of(u, shift, side)
        source = field.at[last, u // 2, :, pl.ds((u % 2) * 128, 128)]

        @pl.when(owner != f)
        def _():
            pltpu.make_async_remote_copy(source, lbuf.at[mine, :], l_send, l_recv, {"fib": owner, "blk": b}, MESH).start()

        @pl.when(owner == f)
        def _():
            pltpu.make_async_copy(source, lbuf.at[mine, :], own_last).start()

    def send_pair(q, _):
        s, zz = lax.div(q, 2), lax.rem(q, 2)
        for peer in fib_peers:
            pltpu.make_async_remote_copy(
                field.at[2 * peer + s, zz], fbuf.at[s, zz, mine, :], a_send, a_recv.at[q], {"fib": peer, "blk": b}, MESH
            ).start()
        return 0

    lax.fori_loop(0, 4, send_pair, 0)

    tiles_x = full_x // 128
    tiles = [(i, j) for i in range(rank // 8) for j in range(tiles_x)]

    def gram_term(fibres):
        projected = jnp.dot(start_t[...], fibres, precision=HIGHEST, preferred_element_type=jnp.float32)
        return lax.dot_general(fibres, projected, NT, precision=HIGHEST, preferred_element_type=jnp.float32)

    extra[...] = jnp.zeros_like(extra)
    own.wait()
    start_copy.wait()
    raw = jnp.zeros((full_x, rank), jnp.float32)
    for q in range(4):
        whole = fbuf.at[q // 2, q % 2]
        pltpu.make_async_copy(whole.at[others, :], whole.at[others, :], a_recv.at[q]).wait()
        raw = raw + gram_term(whole[...])
        if q < 3:
            fhigh[q], flow[q] = halves(whole[...])
        if q == 1:
            @pl.when(is_owner)
            def _():
                pltpu.make_async_copy(lbuf.at[others, :], lbuf.at[others, :], l_recv).wait()
                pltpu.make_async_copy(lbuf.at[mine, :], lbuf.at[mine, :], own_last).wait()
                term = jnp.transpose(gram_term(lbuf[...]))
                for n, (i, j) in enumerate(tiles):
                    extra[n] = term[8 * i : 8 * i + 8, 128 * j : 128 * j + 128]
                lhigh[...], llow[...] = halves(lbuf[...])
    raw_t = jnp.transpose(raw)
    for n, (i, j) in enumerate(tiles):
        part[n] = raw_t[8 * i : 8 * i + 8, 128 * j : 128 * j + 128] + extra[n]

    for other, device in plane_peers:
        pltpu.make_async_remote_copy(part.at[other], rbuf.at[t], r_send, r_recv, device, MESH).start()
    rbuf[t] = part[t]
    fhigh[3], flow[3] = halves(fbuf[1, 1])
    rest = pl.ds(0, plane - 1)
    pltpu.make_async_copy(rbuf.at[rest], rbuf.at[rest], r_recv).wait()
    tile = jnp.sum(rbuf[...], axis=0)
    zsrc[...] = tile
    for device in z_peers:
        pltpu.make_async_remote_copy(zsrc, zbuf.at[z], z_send, z_recv, device, MESH).start()
    zbuf[z] = tile
    rest_z = pl.ds(0, nz - 1)
    pltpu.make_async_copy(zbuf.at[rest_z], zbuf.at[rest_z], z_recv).wait()
    tile = jnp.sum(zbuf[...], axis=0)
    gsrc[...] = tile
    for _, device in plane_peers:
        pltpu.make_async_remote_copy(gsrc, gbuf.at[t], g_send, g_recv, device, MESH).start()
    gbuf[t] = tile
    pltpu.make_async_copy(gbuf.at[rest], gbuf.at[rest], g_recv).wait()
    total_t = jnp.concatenate(
        [jnp.concatenate([gbuf[i * tiles_x + j] for j in range(tiles_x)], axis=1) for i in range(rank // 8)], axis=0)

    def pad(count):
        return [jnp.zeros((count, full_x), jnp.float32)] if count else []

    inner = lax.dot_general(total_t, jnp.concatenate([total_t] + pad(128 - rank), axis=0), NT, precision=HIGHEST,
                            preferred_element_type=jnp.float32)
    inverse = eliminate(inner, rank)
    basis_t = jnp.dot(inverse, jnp.concatenate(pad(rank) + [total_t] + pad(128 - 2 * rank), axis=0), precision=HIGHEST,
                      preferred_element_type=jnp.float32)
    basis_high, basis_low = halves(basis_t)
    basis_both = jnp.concatenate([basis_high, basis_low], axis=0)

    share = rank // nf

    def core_of(high, low):
        both = jnp.dot(basis_both, high, preferred_element_type=jnp.float32)
        return both[:rank] + both[rank:] + jnp.dot(basis_high, low, preferred_element_type=jnp.float32)

    @pl.when(is_owner)
    def _():
        core_part = core_of(lhigh[...], llow[...])
        for j in range(nf):
            lsrc[j] = core_part[share * j : share * j + share, :]

    for q in range(4):
        core_part = core_of(fhigh[q], flow[q])
        for j in range(nf):
            osrc[j, q // 2, q % 2] = core_part[share * j : share * j + share, :]
    target = out.at[pl.ds(2 * f, 2)]
    last_lanes = pl.ds(pl.multiple_of(lax.rem(row_unit, 2) * 128, 128), 128)
    last_target = out.at[last, lax.div(row_unit, 2), :, last_lanes]
    for peer in fib_peers:
        device = {"fib": peer, "blk": b}
        pltpu.make_async_remote_copy(osrc.at[peer], target, o_send, o_recv, device, MESH).start()

        @pl.when(is_owner)
        def _():
            pltpu.make_async_remote_copy(lsrc.at[peer], last_target, p_send, p_recv, device, MESH).start()

    own_core = pltpu.make_async_copy(osrc.at[f], target, own_sem)
    own_core.start()

    @pl.when(is_owner)
    def _():
        own_unit = pltpu.make_async_copy(lsrc.at[f], last_target, own_last)
        own_unit.start()
        own_unit.wait()

    sent = fbuf.at[:, :, others, :]
    pltpu.make_async_copy(sent, sent, a_send).wait()
    pltpu.make_async_copy(rbuf.at[rest], rbuf.at[rest], r_send).wait()
    pltpu.make_async_copy(zbuf.at[rest_z], zbuf.at[rest_z], z_send).wait()
    pltpu.make_async_copy(gbuf.at[rest], gbuf.at[rest], g_send).wait()
    own_core.wait()
    arrived = out.at[pl.ds(0, 2 * (nf - 1))]
    pltpu.make_async_copy(arrived, arrived, o_send).wait()
    pltpu.make_async_copy(arrived, arrived, o_recv).wait()

    def finish_last(units):
        slab = lbuf.at[pl.ds(0, units * width_x), :]
        pltpu.make_async_copy(slab, slab, l_send).wait()
        pltpu.make_async_copy(lsrc.at[pl.ds(0, units)], lsrc.at[pl.ds(0, units)], p_recv).wait()

    @pl.when(is_owner)
    def _():
        finish_last(3)
        pltpu.make_async_copy(lsrc.at[pl.ds(0, nf - 1)], lsrc.at[pl.ds(0, nf - 1)], p_send).wait()

    if side == 4:
        @pl.when(jnp.logical_not(is_owner))
        def _():
            finish_last(4)


def solution(mesh):
    nf, nb = mesh.shape["fib"], mesh.shape["blk"]
    nz = nb // CORES

    def shards(field_data, start_block):
        species, planes, width_x, width_y = field_data.shape
        full_x, rank = start_block.shape
        share = rank // nf
        tiles = rank * full_x // 1024
        assert species == 2 * nf + 1 and planes == 2 and width_y == 256 and tiles == nf * CORES and 2 * rank <= 128
        f32, bf16 = jnp.float32, jnp.bfloat16
        dma = pltpu.SemaphoreType.DMA
        return pl.pallas_call(
            functools.partial(kernel, nf, nz),
            out_shape=jax.ShapeDtypeStruct((species, planes, share, width_y), f32),
            in_specs=[pl.BlockSpec(memory_space=pltpu.HBM), pl.BlockSpec(memory_space=pltpu.HBM)],
            out_specs=pl.BlockSpec(memory_space=pl.ANY),
            scratch_shapes=[
                pltpu.VMEM((rank, full_x), f32),
                pltpu.VMEM((2, 2, full_x, width_y), f32),
                pltpu.VMEM((full_x, 128), f32),
                pltpu.VMEM((4, full_x, width_y), bf16),
                pltpu.VMEM((4, full_x, width_y), bf16),
                pltpu.VMEM((full_x, 128), bf16),
                pltpu.VMEM((full_x, 128), bf16),
                pltpu.VMEM((tiles, 8, 128), f32),
                pltpu.VMEM((tiles, 8, 128), f32),
                pltpu.VMEM((tiles, 8, 128), f32),
                pltpu.VMEM((8, 128), f32),
                pltpu.VMEM((nz, 8, 128), f32),
                pltpu.VMEM((8, 128), f32),
                pltpu.VMEM((tiles, 8, 128), f32),
                pltpu.VMEM((nf, 2, 2, share, width_y), f32),
                pltpu.VMEM((nf, share, 128), f32),
                dma, dma((4,)), dma, dma, dma, dma, dma, dma, dma, dma, dma, dma, dma, dma, dma, dma, dma,
            ],
            compiler_params=pltpu.CompilerParams(collective_id=0, has_side_effects=True, vmem_limit_bytes=48 << 20),
            cost_estimate=pl.CostEstimate(flops=2_000_000_000, bytes_accessed=5_000_000, transcendentals=64),
            name="hosvd_step",
        )(pltpu.with_memory_space_constraint(field_data, pltpu.HBM), pltpu.with_memory_space_constraint(start_block.T, pltpu.HBM))

    in_specs = (P(None, "blk", "fib", None), P())
    out_specs = P(None, "blk", "fib", None)
    return jax.shard_map(shards, mesh=mesh, in_specs=in_specs, out_specs=out_specs, check_vma=False)
```

```python
import functools

import jax
import jax.numpy as jnp
from jax import lax
from jax.experimental import pallas as pl
from jax.experimental.pallas import tpu as pltpu
from jax.sharding import PartitionSpec as P

MESH = pl.DeviceIdType.MESH
HIGHEST = lax.Precision.HIGHEST
CORES = 2
NT = (((1,), (1,)), ((), ()))


def owner_of(unit, shift, side):
    if side == 4:
        return unit * 4 + lax.rem(unit + shift, 4)
    return unit


def ring_distance(step, size):
    return min(step % size, -step % size)


def eliminate(inner, rank):
    wide = inner.shape[1]
    rows = lax.broadcasted_iota(jnp.int32, (rank, wide), 0)
    lanes = lax.broadcasted_iota(jnp.int32, (rank, wide), 1)
    augmented = jnp.where(lanes == rows + rank, 1.0, inner)
    blocks = [augmented[8 * i : 8 * i + 8, :] for i in range(rank // 8)]
    sub = lax.broadcasted_iota(jnp.int32, (8, wide), 0)

    def columns(block, p):
        return [jnp.broadcast_to(block[:, 8 * p + m : 8 * p + m + 1], (8, wide)) for m in range(8)]

    for p in range(rank // 8):
        panel, block = columns(blocks[p], p), blocks[p]
        pivot_rows, factors = [], []
        for j in range(8):
            inv = 1.0 / panel[j][j : j + 1, :]
            pivot_rows.append(block[j : j + 1, :] * inv)
            factors.append([panel[m][j : j + 1, :] * inv for m in range(j + 1, 8)])
            below = jnp.where(sub > j, panel[j], 0.0)
            block = block - below * pivot_rows[j]
            for m in range(j + 1, 8):
                panel[m] = panel[m] - below * factors[j][m - j - 1]
        blocks[p] = block
        for i in range(p + 1, rank // 8):
            panel, block = columns(blocks[i], p), blocks[i]
            for j in range(8):
                block = block - panel[j] * pivot_rows[j]
                for m in range(j + 1, 8):
                    panel[m] = panel[m] - panel[j] * factors[j][m - j - 1]
            blocks[i] = block
    reduced = jnp.concatenate(blocks, axis=0)
    pivots = jnp.sum(jnp.where(lanes == rows, reduced, 0.0), axis=1, keepdims=True)
    return reduced * (1.0 / jnp.sqrt(pivots))


def halves(value):
    high = value.astype(jnp.bfloat16)
    return high, (value - high.astype(jnp.float32)).astype(jnp.bfloat16)


def kernel(nf, nz, field, start_hbm, out, start_t, fbuf, lbuf, fhigh, flow, lhigh, llow, part, extra, rbuf, zsrc, zbuf,
           gsrc, gbuf, osrc, lsrc, a_send, a_recv, own_sem, start_sem, l_send, l_recv, own_last, r_send, r_recv, z_send,
           z_recv, g_send, g_recv, o_send, o_recv, p_send, p_recv):
    side = {16: 4, 4: 2}[nf]
    width_x = field.shape[2]
    rank, full_x = start_t.shape
    last = field.shape[0] - 1
    plane = nf * CORES
    f = lax.axis_index("fib")
    b = lax.axis_index("blk")
    core, z = lax.rem(b, CORES), lax.div(b, CORES)
    t = f * CORES + core
    row, col = lax.div(f, side), lax.rem(f, side)
    shift = lax.rem(b, 4)
    row_unit = row if side == 4 else f
    is_owner = owner_of(row_unit, shift, side) == f
    mine = pl.ds(pl.multiple_of(f * width_x, width_x), width_x)
    others = pl.ds(0, (nf - 1) * width_x)

    own = pltpu.make_async_copy(field.at[pl.ds(2 * f, 2)], fbuf.at[:, :, mine, :], own_sem)
    own.start()
    start_copy = pltpu.make_async_copy(start_hbm, start_t, start_sem)
    start_copy.start()

    steps = [(dy, dx) for dy in range(side) for dx in range(side)]
    steps.sort(key=lambda s: -ring_distance(s[0], side) - ring_distance(s[1], side))
    row_at = [lax.rem(row + d, side) * side for d in range(side)]
    col_at = [lax.rem(col + d, side) for d in range(side)]
    fibs = [row_at[dy] + col_at[dx] for dy, dx in steps]
    fib_peers = fibs[:-1]
    twin = z * CORES + 1 - core
    plane_peers = []
    for other in fibs:
        if other is not fibs[-1]:
            plane_peers.append((other * CORES + core, {"fib": other, "blk": b}))
        plane_peers.append((other * CORES + 1 - core, {"fib": other, "blk": twin}))
    z_steps = sorted(range(1, nz), key=lambda k: -ring_distance(k, nz))
    z_peers = [{"fib": f, "blk": lax.rem(z + k, nz) * CORES + core} for k in z_steps]

    barrier = pltpu.get_barrier_semaphore()
    for _, device in plane_peers:
        pl.semaphore_signal(barrier, inc=1, device_id=device, device_id_type=MESH)
    for device in z_peers:
        pl.semaphore_signal(barrier, inc=1, device_id=device, device_id_type=MESH)
    pl.semaphore_wait(barrier, plane - 1 + nz - 1)

    for u in range(4):
        owner = owner_of(u, shift, side)
        source = field.at[last, u // 2, :, pl.ds((u % 2) * 128, 128)]

        @pl.when(owner != f)
        def _():
            pltpu.make_async_remote_copy(source, lbuf.at[mine, :], l_send, l_recv, {"fib": owner, "blk": b}, MESH).start()

        @pl.when(owner == f)
        def _():
            pltpu.make_async_copy(source, lbuf.at[mine, :], own_last).start()

    def send_pair(q, _):
        s, zz = lax.div(q, 2), lax.rem(q, 2)
        for peer in fib_peers:
            pltpu.make_async_remote_copy(
                field.at[2 * peer + s, zz], fbuf.at[s, zz, mine, :], a_send, a_recv.at[q], {"fib": peer, "blk": b}, MESH
            ).start()
        return 0

    lax.fori_loop(0, 3, send_pair, 0)
    for h in range(2):
        lanes = pl.ds(128 * h, 128)
        for peer in fib_peers:
            pltpu.make_async_remote_copy(
                field.at[2 * peer + 1, 1, :, lanes], fbuf.at[1, 1, mine, lanes], a_send, a_recv.at[3 + h],
                {"fib": peer, "blk": b}, MESH
            ).start()

    tiles_x = full_x // 128
    tiles = [(i, j) for i in range(rank // 8) for j in range(tiles_x)]

    def gram_term(fibres):
        projected = jnp.dot(start_t[...], fibres, precision=HIGHEST, preferred_element_type=jnp.float32)
        return lax.dot_general(projected, fibres, NT, precision=HIGHEST, preferred_element_type=jnp.float32)

    extra[...] = jnp.zeros_like(extra)
    own.wait()
    start_copy.wait()
    chunks = [(0, 0, 0, 256), (0, 1, 0, 256), (1, 0, 0, 256), (1, 1, 0, 128), (1, 1, 128, 128)]
    raw_t = jnp.zeros((rank, full_x), jnp.float32)
    for q, (s, zz, first, width) in enumerate(chunks):
        whole = fbuf.at[s, zz, :, pl.ds(first, width)]
        pltpu.make_async_copy(whole.at[others, :], whole.at[others, :], a_recv.at[q]).wait()
        raw_t = raw_t + gram_term(whole[...])
        if q < 3:
            fhigh[q], flow[q] = halves(whole[...])
        if q == 1:
            @pl.when(is_owner)
            def _():
                pltpu.make_async_copy(lbuf.at[others, :], lbuf.at[others, :], l_recv).wait()
                pltpu.make_async_copy(lbuf.at[mine, :], lbuf.at[mine, :], own_last).wait()
                term = gram_term(lbuf[...])
                for n, (i, j) in enumerate(tiles):
                    extra[n] = term[8 * i : 8 * i + 8, 128 * j : 128 * j + 128]
                lhigh[...], llow[...] = halves(lbuf[...])
        if q == 3:
            for n, (i, j) in enumerate(tiles):
                part[n] = raw_t[8 * i : 8 * i + 8, 128 * j : 128 * j + 128] + extra[n]
            raw_t = jnp.zeros((rank, full_x), jnp.float32)
    for n, (i, j) in enumerate(tiles):
        part[n] += raw_t[8 * i : 8 * i + 8, 128 * j : 128 * j + 128]

    for other, device in plane_peers:
        pltpu.make_async_remote_copy(part.at[other], rbuf.at[t], r_send, r_recv, device, MESH).start()
    rbuf[t] = part[t]
    fhigh[3], flow[3] = halves(fbuf[1, 1])
    rest = pl.ds(0, plane - 1)
    pltpu.make_async_copy(rbuf.at[rest], rbuf.at[rest], r_recv).wait()
    tile = jnp.sum(rbuf[...], axis=0)
    zsrc[...] = tile
    for device in z_peers:
        pltpu.make_async_remote_copy(zsrc, zbuf.at[z], z_send, z_recv, device, MESH).start()
    zbuf[z] = tile
    rest_z = pl.ds(0, nz - 1)
    pltpu.make_async_copy(zbuf.at[rest_z], zbuf.at[rest_z], z_recv).wait()
    tile = jnp.sum(zbuf[...], axis=0)
    gsrc[...] = tile
    for _, device in plane_peers:
        pltpu.make_async_remote_copy(gsrc, gbuf.at[t], g_send, g_recv, device, MESH).start()
    gbuf[t] = tile
    pltpu.make_async_copy(gbuf.at[rest], gbuf.at[rest], g_recv).wait()
    total_t = jnp.concatenate(
        [jnp.concatenate([gbuf[i * tiles_x + j] for j in range(tiles_x)], axis=1) for i in range(rank // 8)], axis=0)

    def pad(count):
        return [jnp.zeros((count, full_x), jnp.float32)] if count else []

    inner = lax.dot_general(total_t, jnp.concatenate([total_t] + pad(128 - rank), axis=0), NT, precision=HIGHEST,
                            preferred_element_type=jnp.float32)
    inverse = eliminate(inner, rank)
    basis_t = jnp.dot(inverse, jnp.concatenate(pad(rank) + [total_t] + pad(128 - 2 * rank), axis=0), precision=HIGHEST,
                      preferred_element_type=jnp.float32)
    basis_high, basis_low = halves(basis_t)
    basis_both = jnp.concatenate([basis_high, basis_low], axis=0)

    share = rank // nf

    def core_of(high, low):
        both = jnp.dot(basis_both, high, preferred_element_type=jnp.float32)
        return both[:rank] + both[rank:] + jnp.dot(basis_high, low, preferred_element_type=jnp.float32)

    @pl.when(is_owner)
    def _():
        core_part = core_of(lhigh[...], llow[...])
        for j in range(nf):
            lsrc[j] = core_part[share * j : share * j + share, :]

    for q in range(4):
        core_part = core_of(fhigh[q], flow[q])
        for j in range(nf):
            osrc[j, q // 2, q % 2] = core_part[share * j : share * j + share, :]
    target = out.at[pl.ds(2 * f, 2)]
    last_lanes = pl.ds(pl.multiple_of(lax.rem(row_unit, 2) * 128, 128), 128)
    last_target = out.at[last, lax.div(row_unit, 2), :, last_lanes]
    for peer in fib_peers:
        device = {"fib": peer, "blk": b}
        pltpu.make_async_remote_copy(osrc.at[peer], target, o_send, o_recv, device, MESH).start()

        @pl.when(is_owner)
        def _():
            pltpu.make_async_remote_copy(lsrc.at[peer], last_target, p_send, p_recv, device, MESH).start()

    own_core = pltpu.make_async_copy(osrc.at[f], target, own_sem)
    own_core.start()

    @pl.when(is_owner)
    def _():
        own_unit = pltpu.make_async_copy(lsrc.at[f], last_target, own_last)
        own_unit.start()
        own_unit.wait()

    sent = fbuf.at[:, :, others, :]
    pltpu.make_async_copy(sent, sent, a_send).wait()
    pltpu.make_async_copy(rbuf.at[rest], rbuf.at[rest], r_send).wait()
    pltpu.make_async_copy(zbuf.at[rest_z], zbuf.at[rest_z], z_send).wait()
    pltpu.make_async_copy(gbuf.at[rest], gbuf.at[rest], g_send).wait()
    own_core.wait()
    arrived = out.at[pl.ds(0, 2 * (nf - 1))]
    pltpu.make_async_copy(arrived, arrived, o_send).wait()
    pltpu.make_async_copy(arrived, arrived, o_recv).wait()

    def finish_last(units):
        slab = lbuf.at[pl.ds(0, units * width_x), :]
        pltpu.make_async_copy(slab, slab, l_send).wait()
        pltpu.make_async_copy(lsrc.at[pl.ds(0, units)], lsrc.at[pl.ds(0, units)], p_recv).wait()

    @pl.when(is_owner)
    def _():
        finish_last(3)
        pltpu.make_async_copy(lsrc.at[pl.ds(0, nf - 1)], lsrc.at[pl.ds(0, nf - 1)], p_send).wait()

    if side == 4:
        @pl.when(jnp.logical_not(is_owner))
        def _():
            finish_last(4)


def solution(mesh):
    nf, nb = mesh.shape["fib"], mesh.shape["blk"]
    nz = nb // CORES

    def shards(field_data, start_block):
        species, planes, width_x, width_y = field_data.shape
        full_x, rank = start_block.shape
        share = rank // nf
        tiles = rank * full_x // 1024
        assert species == 2 * nf + 1 and planes == 2 and width_y == 256 and tiles == nf * CORES and 2 * rank <= 128
        f32, bf16 = jnp.float32, jnp.bfloat16
        dma = pltpu.SemaphoreType.DMA
        return pl.pallas_call(
            functools.partial(kernel, nf, nz),
            out_shape=jax.ShapeDtypeStruct((species, planes, share, width_y), f32),
            in_specs=[pl.BlockSpec(memory_space=pltpu.HBM), pl.BlockSpec(memory_space=pltpu.HBM)],
            out_specs=pl.BlockSpec(memory_space=pl.ANY),
            scratch_shapes=[
                pltpu.VMEM((rank, full_x), f32),
                pltpu.VMEM((2, 2, full_x, width_y), f32),
                pltpu.VMEM((full_x, 128), f32),
                pltpu.VMEM((4, full_x, width_y), bf16),
                pltpu.VMEM((4, full_x, width_y), bf16),
                pltpu.VMEM((full_x, 128), bf16),
                pltpu.VMEM((full_x, 128), bf16),
                pltpu.VMEM((tiles, 8, 128), f32),
                pltpu.VMEM((tiles, 8, 128), f32),
                pltpu.VMEM((tiles, 8, 128), f32),
                pltpu.VMEM((8, 128), f32),
                pltpu.VMEM((nz, 8, 128), f32),
                pltpu.VMEM((8, 128), f32),
                pltpu.VMEM((tiles, 8, 128), f32),
                pltpu.VMEM((nf, 2, 2, share, width_y), f32),
                pltpu.VMEM((nf, share, 128), f32),
                dma, dma((5,)), dma, dma, dma, dma, dma, dma, dma, dma, dma, dma, dma, dma, dma, dma, dma,
            ],
            compiler_params=pltpu.CompilerParams(collective_id=0, has_side_effects=True, vmem_limit_bytes=48 << 20),
            cost_estimate=pl.CostEstimate(flops=2_000_000_000, bytes_accessed=5_000_000, transcendentals=64),
            name="hosvd_step",
        )(pltpu.with_memory_space_constraint(field_data, pltpu.HBM), pltpu.with_memory_space_constraint(start_block.T, pltpu.HBM))

    in_specs = (P(None, "blk", "fib", None), P())
    out_specs = P(None, "blk", "fib", None)
    return jax.shard_map(shards, mesh=mesh, in_specs=in_specs, out_specs=out_specs, check_vma=False)
```

```python
import functools

import jax
import jax.numpy as jnp
from jax import lax
from jax.experimental import pallas as pl
from jax.experimental.pallas import tpu as pltpu
from jax.sharding import PartitionSpec as P

MESH = pl.DeviceIdType.MESH
HIGHEST = lax.Precision.HIGHEST
CORES = 2
NT = (((1,), (1,)), ((), ()))


def owner_of(unit, shift, side):
    if side == 4:
        return unit * 4 + lax.rem(unit + shift, 4)
    return unit


def ring_distance(step, size):
    return min(step % size, -step % size)


def eliminate(inner, rank):
    wide = inner.shape[1]
    rows = lax.broadcasted_iota(jnp.int32, (rank, wide), 0)
    lanes = lax.broadcasted_iota(jnp.int32, (rank, wide), 1)
    augmented = jnp.where(lanes == rows + rank, 1.0, inner)
    blocks = [augmented[8 * i : 8 * i + 8, :] for i in range(rank // 8)]
    sub = lax.broadcasted_iota(jnp.int32, (8, wide), 0)

    def columns(block, p):
        return [jnp.broadcast_to(block[:, 8 * p + m : 8 * p + m + 1], (8, wide)) for m in range(8)]

    for p in range(rank // 8):
        panel, block = columns(blocks[p], p), blocks[p]
        pivot_rows, factors = [], []
        for j in range(8):
            inv = 1.0 / panel[j][j : j + 1, :]
            pivot_rows.append(block[j : j + 1, :] * inv)
            factors.append([panel[m][j : j + 1, :] * inv for m in range(j + 1, 8)])
            below = jnp.where(sub > j, panel[j], 0.0)
            block = block - below * pivot_rows[j]
            for m in range(j + 1, 8):
                panel[m] = panel[m] - below * factors[j][m - j - 1]
        blocks[p] = block
        for i in range(p + 1, rank // 8):
            panel, block = columns(blocks[i], p), blocks[i]
            for j in range(8):
                block = block - panel[j] * pivot_rows[j]
                for m in range(j + 1, 8):
                    panel[m] = panel[m] - panel[j] * factors[j][m - j - 1]
            blocks[i] = block
    reduced = jnp.concatenate(blocks, axis=0)
    pivots = jnp.sum(jnp.where(lanes == rows, reduced, 0.0), axis=1, keepdims=True)
    return reduced * (1.0 / jnp.sqrt(pivots))


def halves(value):
    high = value.astype(jnp.bfloat16)
    return high, (value - high.astype(jnp.float32)).astype(jnp.bfloat16)


def kernel(nf, nz, field, start_hbm, out, start_t, fbuf, lbuf, fhigh, flow, lhigh, llow, part, extra, rbuf, zsrc, zbuf,
           gsrc, gbuf, osrc, lsrc, a_send, a_recv, own_sem, start_sem, l_send, l_recv, own_last, r_send, r_recv, z_send,
           z_recv, g_send, g_recv, o_send, o_recv, p_send, p_recv, plane_in, z_in):
    side = {16: 4, 4: 2}[nf]
    width_x = field.shape[2]
    rank, full_x = start_t.shape
    last = field.shape[0] - 1
    plane = nf * CORES
    f = lax.axis_index("fib")
    b = lax.axis_index("blk")
    core, z = lax.rem(b, CORES), lax.div(b, CORES)
    t = f * CORES + core
    row, col = lax.div(f, side), lax.rem(f, side)
    shift = lax.rem(b, 4)
    row_unit = row if side == 4 else f
    is_owner = owner_of(row_unit, shift, side) == f
    mine = pl.ds(pl.multiple_of(f * width_x, width_x), width_x)
    others = pl.ds(0, (nf - 1) * width_x)

    own = pltpu.make_async_copy(field.at[pl.ds(2 * f, 2)], fbuf.at[:, :, mine, :], own_sem)
    own.start()
    start_copy = pltpu.make_async_copy(start_hbm, start_t, start_sem)
    start_copy.start()

    steps = [(dy, dx) for dy in range(side) for dx in range(side)]
    steps.sort(key=lambda s: -ring_distance(s[0], side) - ring_distance(s[1], side))
    row_at = [lax.rem(row + d, side) * side for d in range(side)]
    col_at = [lax.rem(col + d, side) for d in range(side)]
    fibs = [row_at[dy] + col_at[dx] for dy, dx in steps]
    fib_peers = fibs[:-1]
    twin = z * CORES + 1 - core
    plane_peers = []
    for other in fibs:
        if other is not fibs[-1]:
            plane_peers.append((other * CORES + core, {"fib": other, "blk": b}))
        plane_peers.append((other * CORES + 1 - core, {"fib": other, "blk": twin}))
    z_steps = sorted(range(1, nz), key=lambda k: -ring_distance(k, nz))
    z_peers = [{"fib": f, "blk": lax.rem(z + k, nz) * CORES + core} for k in z_steps]

    barrier = pltpu.get_barrier_semaphore()
    for other in fib_peers:
        pl.semaphore_signal(barrier, inc=1, device_id={"fib": other, "blk": z * CORES}, device_id_type=MESH)

    @pl.when(core == 1)
    def _():
        pl.semaphore_signal(barrier, inc=1, device_id={"fib": f, "blk": z * CORES}, device_id_type=MESH)

    for k in z_steps:
        device = {"fib": f, "blk": lax.rem(z + k, nz) * CORES + 1}
        pl.semaphore_signal(barrier, inc=1, device_id=device, device_id_type=MESH)
    pair = {"fib": f, "blk": twin}

    @pl.when(core == 0)
    def _():
        pl.semaphore_wait(barrier, plane - 1)
        pl.semaphore_signal(plane_in, inc=1, device_id=pair, device_id_type=MESH)

    @pl.when(core == 1)
    def _():
        pl.semaphore_wait(plane_in, 1)

    for u in range(4):
        owner = owner_of(u, shift, side)
        source = field.at[last, u // 2, :, pl.ds((u % 2) * 128, 128)]

        @pl.when(owner != f)
        def _():
            pltpu.make_async_remote_copy(source, lbuf.at[mine, :], l_send, l_recv, {"fib": owner, "blk": b}, MESH).start()

        @pl.when(owner == f)
        def _():
            pltpu.make_async_copy(source, lbuf.at[mine, :], own_last).start()

    def send_pair(q, _):
        s, zz = lax.div(q, 2), lax.rem(q, 2)
        for peer in fib_peers:
            pltpu.make_async_remote_copy(
                field.at[2 * peer + s, zz], fbuf.at[s, zz, mine, :], a_send, a_recv.at[q], {"fib": peer, "blk": b}, MESH
            ).start()
        return 0

    lax.fori_loop(0, 3, send_pair, 0)
    for h in range(2):
        lanes = pl.ds(128 * h, 128)
        for peer in fib_peers:
            pltpu.make_async_remote_copy(
                field.at[2 * peer + 1, 1, :, lanes], fbuf.at[1, 1, mine, lanes], a_send, a_recv.at[3 + h],
                {"fib": peer, "blk": b}, MESH
            ).start()

    tiles_x = full_x // 128
    tiles = [(i, j) for i in range(rank // 8) for j in range(tiles_x)]

    def gram_term(fibres):
        projected = jnp.dot(start_t[...], fibres, precision=HIGHEST, preferred_element_type=jnp.float32)
        return lax.dot_general(projected, fibres, NT, precision=HIGHEST, preferred_element_type=jnp.float32)

    extra[...] = jnp.zeros_like(extra)
    own.wait()
    start_copy.wait()
    chunks = [(0, 0, 0, 256), (0, 1, 0, 256), (1, 0, 0, 256), (1, 1, 0, 128), (1, 1, 128, 128)]
    raw_t = jnp.zeros((rank, full_x), jnp.float32)
    for q, (s, zz, first, width) in enumerate(chunks):
        whole = fbuf.at[s, zz, :, pl.ds(first, width)]
        pltpu.make_async_copy(whole.at[others, :], whole.at[others, :], a_recv.at[q]).wait()
        raw_t = raw_t + gram_term(whole[...])
        if q < 3:
            fhigh[q], flow[q] = halves(whole[...])
        if q == 1:
            @pl.when(is_owner)
            def _():
                pltpu.make_async_copy(lbuf.at[others, :], lbuf.at[others, :], l_recv).wait()
                pltpu.make_async_copy(lbuf.at[mine, :], lbuf.at[mine, :], own_last).wait()
                term = gram_term(lbuf[...])
                for n, (i, j) in enumerate(tiles):
                    extra[n] = term[8 * i : 8 * i + 8, 128 * j : 128 * j + 128]
                lhigh[...], llow[...] = halves(lbuf[...])
        if q == 3:
            for n, (i, j) in enumerate(tiles):
                part[n] = raw_t[8 * i : 8 * i + 8, 128 * j : 128 * j + 128] + extra[n]
            raw_t = jnp.zeros((rank, full_x), jnp.float32)
    for n, (i, j) in enumerate(tiles):
        part[n] += raw_t[8 * i : 8 * i + 8, 128 * j : 128 * j + 128]

    for other, device in plane_peers:
        pltpu.make_async_remote_copy(part.at[other], rbuf.at[t], r_send, r_recv, device, MESH).start()
    rbuf[t] = part[t]
    fhigh[3], flow[3] = halves(fbuf[1, 1])
    rest = pl.ds(0, plane - 1)

    @pl.when(core == 1)
    def _():
        pl.semaphore_wait(barrier, CORES * (nz - 1))
        pl.semaphore_signal(z_in, inc=1, device_id=pair, device_id_type=MESH)

    @pl.when(core == 0)
    def _():
        pl.semaphore_wait(z_in, 1)

    pltpu.make_async_copy(rbuf.at[rest], rbuf.at[rest], r_recv).wait()
    tile = jnp.sum(rbuf[...], axis=0)
    zsrc[...] = tile
    for device in z_peers:
        pltpu.make_async_remote_copy(zsrc, zbuf.at[z], z_send, z_recv, device, MESH).start()
    zbuf[z] = tile
    rest_z = pl.ds(0, nz - 1)
    pltpu.make_async_copy(zbuf.at[rest_z], zbuf.at[rest_z], z_recv).wait()
    tile = jnp.sum(zbuf[...], axis=0)
    gsrc[...] = tile
    for _, device in plane_peers:
        pltpu.make_async_remote_copy(gsrc, gbuf.at[t], g_send, g_recv, device, MESH).start()
    gbuf[t] = tile
    pltpu.make_async_copy(gbuf.at[rest], gbuf.at[rest], g_recv).wait()
    total_t = jnp.concatenate(
        [jnp.concatenate([gbuf[i * tiles_x + j] for j in range(tiles_x)], axis=1) for i in range(rank // 8)], axis=0)

    def pad(count):
        return [jnp.zeros((count, full_x), jnp.float32)] if count else []

    inner = lax.dot_general(total_t, jnp.concatenate([total_t] + pad(128 - rank), axis=0), NT, precision=HIGHEST,
                            preferred_element_type=jnp.float32)
    inverse = eliminate(inner, rank)
    basis_t = jnp.dot(inverse, jnp.concatenate(pad(rank) + [total_t] + pad(128 - 2 * rank), axis=0), precision=HIGHEST,
                      preferred_element_type=jnp.float32)
    basis_high, basis_low = halves(basis_t)
    basis_both = jnp.concatenate([basis_high, basis_low], axis=0)

    share = rank // nf

    def core_of(high, low):
        both = jnp.dot(basis_both, high, preferred_element_type=jnp.float32)
        return both[:rank] + both[rank:] + jnp.dot(basis_high, low, preferred_element_type=jnp.float32)

    @pl.when(is_owner)
    def _():
        core_part = core_of(lhigh[...], llow[...])
        for j in range(nf):
            lsrc[j] = core_part[share * j : share * j + share, :]

    for q in range(4):
        core_part = core_of(fhigh[q], flow[q])
        for j in range(nf):
            osrc[j, q // 2, q % 2] = core_part[share * j : share * j + share, :]
    target = out.at[pl.ds(2 * f, 2)]
    last_lanes = pl.ds(pl.multiple_of(lax.rem(row_unit, 2) * 128, 128), 128)
    last_target = out.at[last, lax.div(row_unit, 2), :, last_lanes]
    for peer in fib_peers:
        device = {"fib": peer, "blk": b}
        pltpu.make_async_remote_copy(osrc.at[peer], target, o_send, o_recv, device, MESH).start()

        @pl.when(is_owner)
        def _():
            pltpu.make_async_remote_copy(lsrc.at[peer], last_target, p_send, p_recv, device, MESH).start()

    own_core = pltpu.make_async_copy(osrc.at[f], target, own_sem)
    own_core.start()

    @pl.when(is_owner)
    def _():
        own_unit = pltpu.make_async_copy(lsrc.at[f], last_target, own_last)
        own_unit.start()
        own_unit.wait()

    sent = fbuf.at[:, :, others, :]
    pltpu.make_async_copy(sent, sent, a_send).wait()
    pltpu.make_async_copy(rbuf.at[rest], rbuf.at[rest], r_send).wait()
    pltpu.make_async_copy(zbuf.at[rest_z], zbuf.at[rest_z], z_send).wait()
    pltpu.make_async_copy(gbuf.at[rest], gbuf.at[rest], g_send).wait()
    own_core.wait()
    arrived = out.at[pl.ds(0, 2 * (nf - 1))]
    pltpu.make_async_copy(arrived, arrived, o_send).wait()
    pltpu.make_async_copy(arrived, arrived, o_recv).wait()

    def finish_last(units):
        slab = lbuf.at[pl.ds(0, units * width_x), :]
        pltpu.make_async_copy(slab, slab, l_send).wait()
        pltpu.make_async_copy(lsrc.at[pl.ds(0, units)], lsrc.at[pl.ds(0, units)], p_recv).wait()

    @pl.when(is_owner)
    def _():
        finish_last(3)
        pltpu.make_async_copy(lsrc.at[pl.ds(0, nf - 1)], lsrc.at[pl.ds(0, nf - 1)], p_send).wait()

    if side == 4:
        @pl.when(jnp.logical_not(is_owner))
        def _():
            finish_last(4)


def solution(mesh):
    nf, nb = mesh.shape["fib"], mesh.shape["blk"]
    nz = nb // CORES

    def shards(field_data, start_block):
        species, planes, width_x, width_y = field_data.shape
        full_x, rank = start_block.shape
        share = rank // nf
        tiles = rank * full_x // 1024
        assert species == 2 * nf + 1 and planes == 2 and width_y == 256 and tiles == nf * CORES and 2 * rank <= 128
        f32, bf16 = jnp.float32, jnp.bfloat16
        dma = pltpu.SemaphoreType.DMA
        return pl.pallas_call(
            functools.partial(kernel, nf, nz),
            out_shape=jax.ShapeDtypeStruct((species, planes, share, width_y), f32),
            in_specs=[pl.BlockSpec(memory_space=pltpu.HBM), pl.BlockSpec(memory_space=pltpu.HBM)],
            out_specs=pl.BlockSpec(memory_space=pl.ANY),
            scratch_shapes=[
                pltpu.VMEM((rank, full_x), f32),
                pltpu.VMEM((2, 2, full_x, width_y), f32),
                pltpu.VMEM((full_x, 128), f32),
                pltpu.VMEM((4, full_x, width_y), bf16),
                pltpu.VMEM((4, full_x, width_y), bf16),
                pltpu.VMEM((full_x, 128), bf16),
                pltpu.VMEM((full_x, 128), bf16),
                pltpu.VMEM((tiles, 8, 128), f32),
                pltpu.VMEM((tiles, 8, 128), f32),
                pltpu.VMEM((tiles, 8, 128), f32),
                pltpu.VMEM((8, 128), f32),
                pltpu.VMEM((nz, 8, 128), f32),
                pltpu.VMEM((8, 128), f32),
                pltpu.VMEM((tiles, 8, 128), f32),
                pltpu.VMEM((nf, 2, 2, share, width_y), f32),
                pltpu.VMEM((nf, share, 128), f32),
                dma, dma((5,)), dma, dma, dma, dma, dma, dma, dma, dma, dma, dma, dma, dma, dma, dma, dma,
                pltpu.SemaphoreType.REGULAR, pltpu.SemaphoreType.REGULAR,
            ],
            compiler_params=pltpu.CompilerParams(collective_id=0, has_side_effects=True, vmem_limit_bytes=48 << 20),
            cost_estimate=pl.CostEstimate(flops=2_000_000_000, bytes_accessed=5_000_000, transcendentals=64),
            name="hosvd_step",
        )(pltpu.with_memory_space_constraint(field_data, pltpu.HBM), pltpu.with_memory_space_constraint(start_block.T, pltpu.HBM))

    in_specs = (P(None, "blk", "fib", None), P())
    out_specs = P(None, "blk", "fib", None)
    return jax.shard_map(shards, mesh=mesh, in_specs=in_specs, out_specs=out_specs, check_vma=False)
```

```python
import functools

import jax
import jax.numpy as jnp
from jax import lax
from jax.experimental import pallas as pl
from jax.experimental.pallas import tpu as pltpu
from jax.sharding import PartitionSpec as P

MESH = pl.DeviceIdType.MESH
HIGHEST = lax.Precision.HIGHEST
CORES = 2
NN = (((1,), (0,)), ((), ()))
NT = (((1,), (1,)), ((), ()))


def owner_of(unit, shift, side):
    if side == 4:
        return unit * 4 + lax.rem(unit + shift, 4)
    return unit


def ring_distance(step, size):
    return min(step % size, -step % size)


def eliminate(inner, rank):
    wide = inner.shape[1]
    rows = lax.broadcasted_iota(jnp.int32, (rank, wide), 0)
    lanes = lax.broadcasted_iota(jnp.int32, (rank, wide), 1)
    augmented = jnp.where(lanes == rows + rank, 1.0, inner)
    blocks = [augmented[8 * i : 8 * i + 8, :] for i in range(rank // 8)]
    sub = lax.broadcasted_iota(jnp.int32, (8, wide), 0)

    def columns(block, p):
        return [jnp.broadcast_to(block[:, 8 * p + m : 8 * p + m + 1], (8, wide)) for m in range(8)]

    for p in range(rank // 8):
        panel, block = columns(blocks[p], p), blocks[p]
        pivot_rows, factors = [], []
        for j in range(8):
            inv = 1.0 / panel[j][j : j + 1, :]
            pivot_rows.append(block[j : j + 1, :] * inv)
            factors.append([panel[m][j : j + 1, :] * inv for m in range(j + 1, 8)])
            below = jnp.where(sub > j, panel[j], 0.0)
            block = block - below * pivot_rows[j]
            for m in range(j + 1, 8):
                panel[m] = panel[m] - below * factors[j][m - j - 1]
        blocks[p] = block
        for i in range(p + 1, rank // 8):
            panel, block = columns(blocks[i], p), blocks[i]
            for j in range(8):
                block = block - panel[j] * pivot_rows[j]
                for m in range(j + 1, 8):
                    panel[m] = panel[m] - panel[j] * factors[j][m - j - 1]
            blocks[i] = block
    reduced = jnp.concatenate(blocks, axis=0)
    pivots = jnp.sum(jnp.where(lanes == rows, reduced, 0.0), axis=1, keepdims=True)
    return reduced * (1.0 / jnp.sqrt(pivots))


def halves(value):
    high = value.astype(jnp.bfloat16)
    return high, (value - high.astype(jnp.float32)).astype(jnp.bfloat16)


def thirds(value):
    high, rest = value.astype(jnp.bfloat16), value
    rest = rest - high.astype(jnp.float32)
    middle = rest.astype(jnp.bfloat16)
    return high, middle, (rest - middle.astype(jnp.float32)).astype(jnp.bfloat16)


def kernel(nf, nz, field, start_hbm, out, start_t, fbuf, lbuf, fparts, lparts, cbuf, part, extra, rbuf, zsrc, zbuf,
           gsrc, gbuf, osrc, lsrc, a_send, a_recv, own_sem, start_sem, l_send, l_recv, own_last, r_send, r_recv, z_send,
           z_recv, g_send, g_recv, o_send, o_recv, p_send, p_recv, plane_in, z_in):
    side = {16: 4, 4: 2}[nf]
    width_x = field.shape[2]
    rank, full_x = start_t.shape
    last = field.shape[0] - 1
    plane = nf * CORES
    f = lax.axis_index("fib")
    b = lax.axis_index("blk")
    core, z = lax.rem(b, CORES), lax.div(b, CORES)
    t = f * CORES + core
    row, col = lax.div(f, side), lax.rem(f, side)
    shift = lax.rem(b, 4)
    row_unit = row if side == 4 else f
    is_owner = owner_of(row_unit, shift, side) == f
    mine = pl.ds(pl.multiple_of(f * width_x, width_x), width_x)
    others = pl.ds(0, (nf - 1) * width_x)

    own = pltpu.make_async_copy(field.at[pl.ds(2 * f, 2)], fbuf.at[:, :, mine, :], own_sem)
    own.start()
    start_copy = pltpu.make_async_copy(start_hbm, start_t, start_sem)
    start_copy.start()

    steps = [(dy, dx) for dy in range(side) for dx in range(side)]
    steps.sort(key=lambda s: -ring_distance(s[0], side) - ring_distance(s[1], side))
    row_at = [lax.rem(row + d, side) * side for d in range(side)]
    col_at = [lax.rem(col + d, side) for d in range(side)]
    fibs = [row_at[dy] + col_at[dx] for dy, dx in steps]
    fib_peers = fibs[:-1]
    twin = z * CORES + 1 - core
    plane_peers = []
    for other in fibs:
        if other is not fibs[-1]:
            plane_peers.append((other * CORES + core, {"fib": other, "blk": b}))
        plane_peers.append((other * CORES + 1 - core, {"fib": other, "blk": twin}))
    z_steps = sorted(range(1, nz), key=lambda k: -ring_distance(k, nz))
    z_peers = [{"fib": f, "blk": lax.rem(z + k, nz) * CORES + core} for k in z_steps]

    barrier = pltpu.get_barrier_semaphore()
    for other in fib_peers:
        pl.semaphore_signal(barrier, inc=1, device_id={"fib": other, "blk": z * CORES}, device_id_type=MESH)

    @pl.when(core == 1)
    def _():
        pl.semaphore_signal(barrier, inc=1, device_id={"fib": f, "blk": z * CORES}, device_id_type=MESH)

    for k in z_steps:
        device = {"fib": f, "blk": lax.rem(z + k, nz) * CORES + 1}
        pl.semaphore_signal(barrier, inc=1, device_id=device, device_id_type=MESH)
    pair = {"fib": f, "blk": twin}

    @pl.when(core == 0)
    def _():
        pl.semaphore_wait(barrier, plane - 1)
        pl.semaphore_signal(plane_in, inc=1, device_id=pair, device_id_type=MESH)

    @pl.when(core == 1)
    def _():
        pl.semaphore_wait(plane_in, 1)

    for u in range(4):
        owner = owner_of(u, shift, side)
        source = field.at[last, u // 2, :, pl.ds((u % 2) * 128, 128)]

        @pl.when(owner != f)
        def _():
            pltpu.make_async_remote_copy(source, lbuf.at[mine, :], l_send, l_recv, {"fib": owner, "blk": b}, MESH).start()

        @pl.when(owner == f)
        def _():
            pltpu.make_async_copy(source, lbuf.at[mine, :], own_last).start()

    def send_pair(q, _):
        s, zz = lax.div(q, 2), lax.rem(q, 2)
        for peer in fib_peers:
            pltpu.make_async_remote_copy(
                field.at[2 * peer + s, zz], fbuf.at[s, zz, mine, :], a_send, a_recv.at[q], {"fib": peer, "blk": b}, MESH
            ).start()
        return 0

    lax.fori_loop(0, 3, send_pair, 0)
    for h in range(2):
        lanes = pl.ds(128 * h, 128)
        for peer in fib_peers:
            pltpu.make_async_remote_copy(
                field.at[2 * peer + 1, 1, :, lanes], fbuf.at[1, 1, mine, lanes], a_send, a_recv.at[3 + h],
                {"fib": peer, "blk": b}, MESH
            ).start()

    tiles_x = full_x // 128
    tiles = [(i, j) for i in range(rank // 8) for j in range(tiles_x)]

    def gram_term(fibres):
        projected = jnp.dot(start_t[...], fibres, precision=HIGHEST, preferred_element_type=jnp.float32)
        return lax.dot_general(projected, fibres, NT, precision=HIGHEST, preferred_element_type=jnp.float32)

    def times_halves(left, high, low, dims):
        left_high, left_low = halves(left)
        both = lax.dot_general(jnp.concatenate([left_high, left_low], axis=0), high, dims,
                               preferred_element_type=jnp.float32)
        return both[:rank] + both[rank:] + lax.dot_general(left_high, low, dims, preferred_element_type=jnp.float32)

    def gram_term_halves(fibres):
        high, low = halves(fibres)
        projected = times_halves(start_t[...], high, low, NN)
        return times_halves(projected, high, low, NT)

    extra[...] = jnp.zeros_like(extra)
    lparts[...] = jnp.zeros_like(lparts)
    own.wait()
    start_copy.wait()
    chunks = [(0, 0, 0, 256), (0, 1, 0, 256), (1, 0, 0, 256), (1, 1, 0, 128), (1, 1, 128, 128)]
    raw_t = jnp.zeros((rank, full_x), jnp.float32)
    for q, (s, zz, first, width) in enumerate(chunks):
        whole = fbuf.at[s, zz, :, pl.ds(first, width)]
        pltpu.make_async_copy(whole.at[others, :], whole.at[others, :], a_recv.at[q]).wait()
        if q < 4:
            raw_t = raw_t + gram_term(whole[...])
        else:
            raw_t = gram_term_halves(whole[...])
        if q < 3:
            fparts[q, 0], fparts[q, 1], fparts[q, 2] = thirds(whole[...])
        if q == 1:
            @pl.when(is_owner)
            def _():
                pltpu.make_async_copy(lbuf.at[others, :], lbuf.at[others, :], l_recv).wait()
                pltpu.make_async_copy(lbuf.at[mine, :], lbuf.at[mine, :], own_last).wait()
                term = gram_term(lbuf[...])
                for n, (i, j) in enumerate(tiles):
                    extra[n] = term[8 * i : 8 * i + 8, 128 * j : 128 * j + 128]
                lparts[0], lparts[1], lparts[2] = thirds(lbuf[...])
        if q == 3:
            for n, (i, j) in enumerate(tiles):
                part[n] = raw_t[8 * i : 8 * i + 8, 128 * j : 128 * j + 128] + extra[n]
    for n, (i, j) in enumerate(tiles):
        part[n] += raw_t[8 * i : 8 * i + 8, 128 * j : 128 * j + 128]

    for other, device in plane_peers:
        pltpu.make_async_remote_copy(part.at[other], rbuf.at[t], r_send, r_recv, device, MESH).start()
    rbuf[t] = part[t]
    fparts[3, 0], fparts[3, 1], fparts[3, 2] = thirds(fbuf[1, 1])
    rest = pl.ds(0, plane - 1)

    @pl.when(core == 1)
    def _():
        pl.semaphore_wait(barrier, CORES * (nz - 1))
        pl.semaphore_signal(z_in, inc=1, device_id=pair, device_id_type=MESH)

    @pl.when(core == 0)
    def _():
        pl.semaphore_wait(z_in, 1)

    pltpu.make_async_copy(rbuf.at[rest], rbuf.at[rest], r_recv).wait()
    tile = jnp.sum(rbuf[...], axis=0)
    zsrc[...] = tile
    for device in z_peers:
        pltpu.make_async_remote_copy(zsrc, zbuf.at[z], z_send, z_recv, device, MESH).start()
    zbuf[z] = tile
    rest_z = pl.ds(0, nz - 1)
    pltpu.make_async_copy(zbuf.at[rest_z], zbuf.at[rest_z], z_recv).wait()
    tile = jnp.sum(zbuf[...], axis=0)
    gsrc[...] = tile
    for _, device in plane_peers:
        pltpu.make_async_remote_copy(gsrc, gbuf.at[t], g_send, g_recv, device, MESH).start()
    gbuf[t] = tile
    pltpu.make_async_copy(gbuf.at[rest], gbuf.at[rest], g_recv).wait()
    total_t = jnp.concatenate(
        [jnp.concatenate([gbuf[i * tiles_x + j] for j in range(tiles_x)], axis=1) for i in range(rank // 8)], axis=0)

    share = rank // nf
    high, middle, low = thirds(total_t)
    stack = jnp.concatenate([high, middle, low], axis=0)

    def products(parts):
        first = jnp.dot(stack, parts[0], preferred_element_type=jnp.float32)
        second = jnp.dot(stack[: 2 * rank], parts[1], preferred_element_type=jnp.float32)
        third = jnp.dot(high, parts[2], preferred_element_type=jnp.float32)
        return first[:rank] + (second[:rank] + first[rank : 2 * rank]) + (
            third + second[rank:] + first[2 * rank :])

    padding = jnp.zeros((128 - rank, full_x), jnp.float32)
    inner = lax.dot_general(total_t, jnp.concatenate([total_t, padding], axis=0), NT, precision=HIGHEST,
                            preferred_element_type=jnp.float32)
    for q in range(4):
        cbuf[:, 256 * q : 256 * q + 256] = products(fparts[q])
    cbuf[:, 1024:] = products(lparts[...])
    inverse = eliminate(inner, rank)

    def core_of(lanes, width):
        pieces = [jnp.zeros((rank, width), jnp.float32), cbuf[:, lanes]]
        if 128 - 2 * rank:
            pieces.append(jnp.zeros((128 - 2 * rank, width), jnp.float32))
        return jnp.dot(inverse, jnp.concatenate(pieces, axis=0), precision=HIGHEST, preferred_element_type=jnp.float32)

    for q in range(4):
        core_part = core_of(pl.ds(256 * q, 256), 256)
        for j in range(nf):
            osrc[j, q // 2, q % 2] = core_part[share * j : share * j + share, :]
    core_part = core_of(pl.ds(1024, 128), 128)
    for j in range(nf):
        lsrc[j] = core_part[share * j : share * j + share, :]
    target = out.at[pl.ds(2 * f, 2)]
    last_lanes = pl.ds(pl.multiple_of(lax.rem(row_unit, 2) * 128, 128), 128)
    last_target = out.at[last, lax.div(row_unit, 2), :, last_lanes]
    for peer in fib_peers:
        device = {"fib": peer, "blk": b}
        pltpu.make_async_remote_copy(osrc.at[peer], target, o_send, o_recv, device, MESH).start()

        @pl.when(is_owner)
        def _():
            pltpu.make_async_remote_copy(lsrc.at[peer], last_target, p_send, p_recv, device, MESH).start()

    own_core = pltpu.make_async_copy(osrc.at[f], target, own_sem)
    own_core.start()

    @pl.when(is_owner)
    def _():
        own_unit = pltpu.make_async_copy(lsrc.at[f], last_target, own_last)
        own_unit.start()
        own_unit.wait()

    sent = fbuf.at[:, :, others, :]
    pltpu.make_async_copy(sent, sent, a_send).wait()
    pltpu.make_async_copy(rbuf.at[rest], rbuf.at[rest], r_send).wait()
    pltpu.make_async_copy(zbuf.at[rest_z], zbuf.at[rest_z], z_send).wait()
    pltpu.make_async_copy(gbuf.at[rest], gbuf.at[rest], g_send).wait()
    own_core.wait()
    arrived = out.at[pl.ds(0, 2 * (nf - 1))]
    pltpu.make_async_copy(arrived, arrived, o_send).wait()
    pltpu.make_async_copy(arrived, arrived, o_recv).wait()

    def finish_last(units):
        slab = lbuf.at[pl.ds(0, units * width_x), :]
        pltpu.make_async_copy(slab, slab, l_send).wait()
        pltpu.make_async_copy(lsrc.at[pl.ds(0, units)], lsrc.at[pl.ds(0, units)], p_recv).wait()

    @pl.when(is_owner)
    def _():
        finish_last(3)
        pltpu.make_async_copy(lsrc.at[pl.ds(0, nf - 1)], lsrc.at[pl.ds(0, nf - 1)], p_send).wait()

    if side == 4:
        @pl.when(jnp.logical_not(is_owner))
        def _():
            finish_last(4)


def solution(mesh):
    nf, nb = mesh.shape["fib"], mesh.shape["blk"]
    nz = nb // CORES

    def shards(field_data, start_block):
        species, planes, width_x, width_y = field_data.shape
        full_x, rank = start_block.shape
        share = rank // nf
        tiles = rank * full_x // 1024
        assert species == 2 * nf + 1 and planes == 2 and width_y == 256 and tiles == nf * CORES and 2 * rank <= 128
        f32, bf16 = jnp.float32, jnp.bfloat16
        dma = pltpu.SemaphoreType.DMA
        return pl.pallas_call(
            functools.partial(kernel, nf, nz),
            out_shape=jax.ShapeDtypeStruct((species, planes, share, width_y), f32),
            in_specs=[pl.BlockSpec(memory_space=pltpu.HBM), pl.BlockSpec(memory_space=pltpu.HBM)],
            out_specs=pl.BlockSpec(memory_space=pl.ANY),
            scratch_shapes=[
                pltpu.VMEM((rank, full_x), f32),
                pltpu.VMEM((2, 2, full_x, width_y), f32),
                pltpu.VMEM((full_x, 128), f32),
                pltpu.VMEM((4, 3, full_x, width_y), bf16),
                pltpu.VMEM((3, full_x, 128), bf16),
                pltpu.VMEM((rank, 4 * width_y + 128), f32),
                pltpu.VMEM((tiles, 8, 128), f32),
                pltpu.VMEM((tiles, 8, 128), f32),
                pltpu.VMEM((tiles, 8, 128), f32),
                pltpu.VMEM((8, 128), f32),
                pltpu.VMEM((nz, 8, 128), f32),
                pltpu.VMEM((8, 128), f32),
                pltpu.VMEM((tiles, 8, 128), f32),
                pltpu.VMEM((nf, 2, 2, share, width_y), f32),
                pltpu.VMEM((nf, share, 128), f32),
                dma, dma((5,)), dma, dma, dma, dma, dma, dma, dma, dma, dma, dma, dma, dma, dma, dma, dma,
                pltpu.SemaphoreType.REGULAR, pltpu.SemaphoreType.REGULAR,
            ],
            compiler_params=pltpu.CompilerParams(collective_id=0, has_side_effects=True, vmem_limit_bytes=48 << 20),
            cost_estimate=pl.CostEstimate(flops=2_000_000_000, bytes_accessed=5_000_000, transcendentals=64),
            name="hosvd_step",
        )(pltpu.with_memory_space_constraint(field_data, pltpu.HBM), pltpu.with_memory_space_constraint(start_block.T, pltpu.HBM))

    in_specs = (P(None, "blk", "fib", None), P())
    out_specs = P(None, "blk", "fib", None)
    return jax.shard_map(shards, mesh=mesh, in_specs=in_specs, out_specs=out_specs, check_vma=False)
```

```python
import functools

import jax
import jax.numpy as jnp
from jax import lax
from jax.experimental import pallas as pl
from jax.experimental.pallas import tpu as pltpu
from jax.sharding import PartitionSpec as P

MESH = pl.DeviceIdType.MESH
HIGHEST = lax.Precision.HIGHEST
CORES = 2
NN = (((1,), (0,)), ((), ()))
NT = (((1,), (1,)), ((), ()))


def owner_of(unit, shift, side):
    if side == 4:
        return unit * 4 + lax.rem(unit + shift, 4)
    return unit


def ring_distance(step, size):
    return min(step % size, -step % size)


def eliminate(inner, rank):
    wide = inner.shape[1]
    rows = lax.broadcasted_iota(jnp.int32, (rank, wide), 0)
    lanes = lax.broadcasted_iota(jnp.int32, (rank, wide), 1)
    augmented = jnp.where(lanes == rows + rank, 1.0, inner)
    blocks = [augmented[8 * i : 8 * i + 8, :] for i in range(rank // 8)]
    sub = lax.broadcasted_iota(jnp.int32, (8, wide), 0)

    def columns(block, p):
        return [jnp.broadcast_to(block[:, 8 * p + m : 8 * p + m + 1], (8, wide)) for m in range(8)]

    for p in range(rank // 8):
        panel, block = columns(blocks[p], p), blocks[p]
        pivot_rows, factors = [], []
        for j in range(8):
            inv = 1.0 / panel[j][j : j + 1, :]
            pivot_rows.append(block[j : j + 1, :] * inv)
            factors.append([panel[m][j : j + 1, :] * inv for m in range(j + 1, 8)])
            below = jnp.where(sub > j, panel[j], 0.0)
            block = block - below * pivot_rows[j]
            for m in range(j + 1, 8):
                panel[m] = panel[m] - below * factors[j][m - j - 1]
        blocks[p] = block
        for i in range(p + 1, rank // 8):
            panel, block = columns(blocks[i], p), blocks[i]
            for j in range(8):
                block = block - panel[j] * pivot_rows[j]
                for m in range(j + 1, 8):
                    panel[m] = panel[m] - panel[j] * factors[j][m - j - 1]
            blocks[i] = block
    reduced = jnp.concatenate(blocks, axis=0)
    pivots = jnp.sum(jnp.where(lanes == rows, reduced, 0.0), axis=1, keepdims=True)
    return reduced * (1.0 / jnp.sqrt(pivots))


def halves(value):
    high = value.astype(jnp.bfloat16)
    return high, (value - high.astype(jnp.float32)).astype(jnp.bfloat16)


def thirds(value):
    high, rest = value.astype(jnp.bfloat16), value
    rest = rest - high.astype(jnp.float32)
    middle = rest.astype(jnp.bfloat16)
    return high, middle, (rest - middle.astype(jnp.float32)).astype(jnp.bfloat16)


def kernel(nf, nz, field, start_hbm, out, start_t, fbuf, lbuf, fparts, lparts, cparts, part, extra, rbuf, zsrc, zbuf,
           gsrc, gbuf, osrc, lsrc, a_send, a_recv, own_sem, start_sem, l_send, l_recv, own_last, r_send, r_recv, z_send,
           z_recv, g_send, g_recv, o_send, o_recv, p_send, p_recv, plane_in, z_in):
    side = {16: 4, 4: 2}[nf]
    width_x = field.shape[2]
    rank, full_x = start_t.shape
    last = field.shape[0] - 1
    plane = nf * CORES
    f = lax.axis_index("fib")
    b = lax.axis_index("blk")
    core, z = lax.rem(b, CORES), lax.div(b, CORES)
    t = f * CORES + core
    row, col = lax.div(f, side), lax.rem(f, side)
    shift = lax.rem(b, 4)
    row_unit = row if side == 4 else f
    is_owner = owner_of(row_unit, shift, side) == f
    mine = pl.ds(pl.multiple_of(f * width_x, width_x), width_x)
    others = pl.ds(0, (nf - 1) * width_x)

    steps = [(dy, dx) for dy in range(side) for dx in range(side)]
    steps.sort(key=lambda s: -ring_distance(s[0], side) - ring_distance(s[1], side))
    row_at = [lax.rem(row + d, side) * side for d in range(side)]
    col_at = [lax.rem(col + d, side) for d in range(side)]
    fibs = [row_at[dy] + col_at[dx] for dy, dx in steps]
    fib_peers = fibs[:-1]
    twin = z * CORES + 1 - core
    plane_peers = []
    for other in fibs:
        if other is not fibs[-1]:
            plane_peers.append((other * CORES + core, {"fib": other, "blk": b}))
        plane_peers.append((other * CORES + 1 - core, {"fib": other, "blk": twin}))
    z_steps = sorted(range(1, nz), key=lambda k: -ring_distance(k, nz))
    z_peers = [{"fib": f, "blk": lax.rem(z + k, nz) * CORES + core} for k in z_steps]

    barrier = pltpu.get_barrier_semaphore()
    for other in fib_peers:
        pl.semaphore_signal(barrier, inc=1, device_id={"fib": other, "blk": z * CORES}, device_id_type=MESH)

    @pl.when(core == 1)
    def _():
        pl.semaphore_signal(barrier, inc=1, device_id={"fib": f, "blk": z * CORES}, device_id_type=MESH)

    for k in z_steps:
        device = {"fib": f, "blk": lax.rem(z + k, nz) * CORES + 1}
        pl.semaphore_signal(barrier, inc=1, device_id=device, device_id_type=MESH)
    pair = {"fib": f, "blk": twin}

    own = pltpu.make_async_copy(field.at[pl.ds(2 * f, 2)], fbuf.at[:, :, mine, :], own_sem)
    own.start()
    start_copy = pltpu.make_async_copy(start_hbm, start_t, start_sem)
    start_copy.start()

    @pl.when(core == 0)
    def _():
        pl.semaphore_wait(barrier, plane - 1)
        pl.semaphore_signal(plane_in, inc=1, device_id=pair, device_id_type=MESH)

    @pl.when(core == 1)
    def _():
        pl.semaphore_wait(plane_in, 1)

    def send_pair(q, _):
        s, zz = lax.div(q, 2), lax.rem(q, 2)
        for peer in fib_peers:
            pltpu.make_async_remote_copy(
                field.at[2 * peer + s, zz], fbuf.at[s, zz, mine, :], a_send, a_recv.at[q], {"fib": peer, "blk": b}, MESH
            ).start()
        return 0

    send_pair(0, 0)
    for u in range(4):
        owner = owner_of(u, shift, side)
        source = field.at[last, u // 2, :, pl.ds((u % 2) * 128, 128)]

        @pl.when(owner != f)
        def _():
            pltpu.make_async_remote_copy(source, lbuf.at[mine, :], l_send, l_recv, {"fib": owner, "blk": b}, MESH).start()

        @pl.when(owner == f)
        def _():
            pltpu.make_async_copy(source, lbuf.at[mine, :], own_last).start()

    lax.fori_loop(1, 3, send_pair, 0)
    for h in range(2):
        lanes = pl.ds(128 * h, 128)
        for peer in fib_peers:
            pltpu.make_async_remote_copy(
                field.at[2 * peer + 1, 1, :, lanes], fbuf.at[1, 1, mine, lanes], a_send, a_recv.at[3 + h],
                {"fib": peer, "blk": b}, MESH
            ).start()

    tiles_x = full_x // 128
    tiles = [(i, j) for i in range(rank // 8) for j in range(tiles_x)]

    def gram_term(fibres):
        projected = jnp.dot(start_t[...], fibres, precision=HIGHEST, preferred_element_type=jnp.float32)
        return lax.dot_general(projected, fibres, NT, precision=HIGHEST, preferred_element_type=jnp.float32)

    def times_halves(left, high, low, dims):
        left_high, left_low = halves(left)
        both = lax.dot_general(jnp.concatenate([left_high, left_low], axis=0), high, dims,
                               preferred_element_type=jnp.float32)
        return both[:rank] + both[rank:] + lax.dot_general(left_high, low, dims, preferred_element_type=jnp.float32)

    def gram_term_halves(fibres):
        high, low = halves(fibres)
        projected = times_halves(start_t[...], high, low, NN)
        return times_halves(projected, high, low, NT)

    extra[...] = jnp.zeros_like(extra)
    lparts[...] = jnp.zeros_like(lparts)
    cparts[...] = jnp.zeros_like(cparts)
    own.wait()
    start_copy.wait()
    chunks = [(0, 0, 0, 256), (0, 1, 0, 256), (1, 0, 0, 256), (1, 1, 0, 128), (1, 1, 128, 128)]
    raw_t = jnp.zeros((rank, full_x), jnp.float32)
    for q, (s, zz, first, width) in enumerate(chunks):
        whole = fbuf.at[s, zz, :, pl.ds(first, width)]
        pltpu.make_async_copy(whole.at[others, :], whole.at[others, :], a_recv.at[q]).wait()
        if q < 4:
            raw_t = raw_t + gram_term(whole[...])
        else:
            raw_t = gram_term_halves(whole[...])
        if q < 3:
            fparts[q, 0], fparts[q, 1], fparts[q, 2] = thirds(whole[...])
        if q == 1:
            @pl.when(is_owner)
            def _():
                pltpu.make_async_copy(lbuf.at[others, :], lbuf.at[others, :], l_recv).wait()
                pltpu.make_async_copy(lbuf.at[mine, :], lbuf.at[mine, :], own_last).wait()
                term = gram_term(lbuf[...])
                for n, (i, j) in enumerate(tiles):
                    extra[n] = term[8 * i : 8 * i + 8, 128 * j : 128 * j + 128]
                lparts[0], lparts[1], lparts[2] = thirds(lbuf[...])
        if q == 3:
            for n, (i, j) in enumerate(tiles):
                part[n] = raw_t[8 * i : 8 * i + 8, 128 * j : 128 * j + 128] + extra[n]
    for n, (i, j) in enumerate(tiles):
        part[n] += raw_t[8 * i : 8 * i + 8, 128 * j : 128 * j + 128]

    for other, device in plane_peers:
        pltpu.make_async_remote_copy(part.at[other], rbuf.at[t], r_send, r_recv, device, MESH).start()
    rbuf[t] = part[t]
    fparts[3, 0], fparts[3, 1], fparts[3, 2] = thirds(fbuf[1, 1])
    rest = pl.ds(0, plane - 1)

    @pl.when(core == 1)
    def _():
        pl.semaphore_wait(barrier, CORES * (nz - 1))
        pl.semaphore_signal(z_in, inc=1, device_id=pair, device_id_type=MESH)

    @pl.when(core == 0)
    def _():
        pl.semaphore_wait(z_in, 1)

    pltpu.make_async_copy(rbuf.at[rest], rbuf.at[rest], r_recv).wait()
    tile = jnp.sum(rbuf[...], axis=0)
    zsrc[...] = tile
    for device in z_peers:
        pltpu.make_async_remote_copy(zsrc, zbuf.at[z], z_send, z_recv, device, MESH).start()
    zbuf[z] = tile
    rest_z = pl.ds(0, nz - 1)
    pltpu.make_async_copy(zbuf.at[rest_z], zbuf.at[rest_z], z_recv).wait()
    tile = jnp.sum(zbuf[...], axis=0)
    gsrc[...] = tile
    for _, device in plane_peers:
        pltpu.make_async_remote_copy(gsrc, gbuf.at[t], g_send, g_recv, device, MESH).start()
    gbuf[t] = tile
    pltpu.make_async_copy(gbuf.at[rest], gbuf.at[rest], g_recv).wait()
    total_t = jnp.concatenate(
        [jnp.concatenate([gbuf[i * tiles_x + j] for j in range(tiles_x)], axis=1) for i in range(rank // 8)], axis=0)

    share = rank // nf
    high, middle, low = thirds(total_t)
    stack = jnp.concatenate([high, middle, low], axis=0)

    def products(parts, dims=NN, stack=stack):
        first = lax.dot_general(stack, parts[0], dims, preferred_element_type=jnp.float32)
        second = lax.dot_general(stack[: 2 * rank], parts[1], dims, preferred_element_type=jnp.float32)
        third = lax.dot_general(stack[:rank], parts[2], dims, preferred_element_type=jnp.float32)
        return first[:rank] + (second[:rank] + first[rank : 2 * rank]) + (
            third + second[rank:] + first[2 * rank :])

    padding = jnp.zeros((128 - rank, full_x), jnp.float32)
    zeros_right = padding.astype(jnp.bfloat16)
    wide = [jnp.concatenate([value, zeros_right], axis=0) for value in (high, middle, low)]
    inner = products(wide, NT)
    for q in range(4):
        cparts[:, rank : 2 * rank, 256 * q : 256 * q + 256] = jnp.stack(thirds(products(fparts[q])))
    cparts[:, rank : 2 * rank, 1024:] = jnp.stack(thirds(products(lparts[...])))
    inverse = jnp.concatenate(thirds(eliminate(inner, rank)), axis=0)

    def core_of(lanes):
        return products(cparts[:, :, lanes], NN, inverse)

    for q in range(4):
        core_part = core_of(pl.ds(256 * q, 256))
        for j in range(nf):
            osrc[j, q // 2, q % 2] = core_part[share * j : share * j + share, :]
    core_part = core_of(pl.ds(1024, 128))
    for j in range(nf):
        lsrc[j] = core_part[share * j : share * j + share, :]
    target = out.at[pl.ds(2 * f, 2)]
    last_lanes = pl.ds(pl.multiple_of(lax.rem(row_unit, 2) * 128, 128), 128)
    last_target = out.at[last, lax.div(row_unit, 2), :, last_lanes]
    for peer in fib_peers:
        device = {"fib": peer, "blk": b}
        pltpu.make_async_remote_copy(osrc.at[peer], target, o_send, o_recv, device, MESH).start()

        @pl.when(is_owner)
        def _():
            pltpu.make_async_remote_copy(lsrc.at[peer], last_target, p_send, p_recv, device, MESH).start()

    own_core = pltpu.make_async_copy(osrc.at[f], target, own_sem)
    own_core.start()

    @pl.when(is_owner)
    def _():
        own_unit = pltpu.make_async_copy(lsrc.at[f], last_target, own_last)
        own_unit.start()
        own_unit.wait()

    sent = fbuf.at[:, :, others, :]
    pltpu.make_async_copy(sent, sent, a_send).wait()
    pltpu.make_async_copy(rbuf.at[rest], rbuf.at[rest], r_send).wait()
    pltpu.make_async_copy(zbuf.at[rest_z], zbuf.at[rest_z], z_send).wait()
    pltpu.make_async_copy(gbuf.at[rest], gbuf.at[rest], g_send).wait()
    own_core.wait()
    arrived = out.at[pl.ds(0, 2 * (nf - 1))]
    pltpu.make_async_copy(arrived, arrived, o_send).wait()
    pltpu.make_async_copy(arrived, arrived, o_recv).wait()

    def finish_last(units):
        slab = lbuf.at[pl.ds(0, units * width_x), :]
        pltpu.make_async_copy(slab, slab, l_send).wait()
        pltpu.make_async_copy(lsrc.at[pl.ds(0, units)], lsrc.at[pl.ds(0, units)], p_recv).wait()

    @pl.when(is_owner)
    def _():
        finish_last(3)
        pltpu.make_async_copy(lsrc.at[pl.ds(0, nf - 1)], lsrc.at[pl.ds(0, nf - 1)], p_send).wait()

    if side == 4:
        @pl.when(jnp.logical_not(is_owner))
        def _():
            finish_last(4)


def solution(mesh):
    nf, nb = mesh.shape["fib"], mesh.shape["blk"]
    nz = nb // CORES

    def shards(field_data, start_block):
        species, planes, width_x, width_y = field_data.shape
        full_x, rank = start_block.shape
        share = rank // nf
        tiles = rank * full_x // 1024
        assert species == 2 * nf + 1 and planes == 2 and width_y == 256 and tiles == nf * CORES and 2 * rank <= 128
        f32, bf16 = jnp.float32, jnp.bfloat16
        dma = pltpu.SemaphoreType.DMA
        return pl.pallas_call(
            functools.partial(kernel, nf, nz),
            out_shape=jax.ShapeDtypeStruct((species, planes, share, width_y), f32),
            in_specs=[pl.BlockSpec(memory_space=pltpu.HBM), pl.BlockSpec(memory_space=pltpu.HBM)],
            out_specs=pl.BlockSpec(memory_space=pl.ANY),
            scratch_shapes=[
                pltpu.VMEM((rank, full_x), f32),
                pltpu.VMEM((2, 2, full_x, width_y), f32),
                pltpu.VMEM((full_x, 128), f32),
                pltpu.VMEM((4, 3, full_x, width_y), bf16),
                pltpu.VMEM((3, full_x, 128), bf16),
                pltpu.VMEM((3, 128, 4 * width_y + 128), bf16),
                pltpu.VMEM((tiles, 8, 128), f32),
                pltpu.VMEM((tiles, 8, 128), f32),
                pltpu.VMEM((tiles, 8, 128), f32),
                pltpu.VMEM((8, 128), f32),
                pltpu.VMEM((nz, 8, 128), f32),
                pltpu.VMEM((8, 128), f32),
                pltpu.VMEM((tiles, 8, 128), f32),
                pltpu.VMEM((nf, 2, 2, share, width_y), f32),
                pltpu.VMEM((nf, share, 128), f32),
                dma, dma((5,)), dma, dma, dma, dma, dma, dma, dma, dma, dma, dma, dma, dma, dma, dma, dma,
                pltpu.SemaphoreType.REGULAR, pltpu.SemaphoreType.REGULAR,
            ],
            compiler_params=pltpu.CompilerParams(collective_id=0, has_side_effects=True, vmem_limit_bytes=48 << 20),
            cost_estimate=pl.CostEstimate(flops=2_000_000_000, bytes_accessed=5_000_000, transcendentals=64),
            name="hosvd_step",
        )(pltpu.with_memory_space_constraint(field_data, pltpu.HBM), pltpu.with_memory_space_constraint(start_block.T, pltpu.HBM))

    in_specs = (P(None, "blk", "fib", None), P())
    out_specs = P(None, "blk", "fib", None)
    return jax.shard_map(shards, mesh=mesh, in_specs=in_specs, out_specs=out_specs, check_vma=False)
```

```python
import functools

import jax
import jax.numpy as jnp
from jax import lax
from jax.experimental import pallas as pl
from jax.experimental.pallas import tpu as pltpu
from jax.sharding import PartitionSpec as P

MESH = pl.DeviceIdType.MESH
HIGHEST = lax.Precision.HIGHEST
CORES = 2
NN = (((1,), (0,)), ((), ()))
NT = (((1,), (1,)), ((), ()))


def owner_of(unit, shift, side):
    if side == 4:
        return unit * 4 + lax.rem(unit + shift, 4)
    return unit


def ring_distance(step, size):
    return min(step % size, -step % size)


def eliminate(inner, rank):
    wide = inner.shape[1]
    rows = lax.broadcasted_iota(jnp.int32, (rank, wide), 0)
    lanes = lax.broadcasted_iota(jnp.int32, (rank, wide), 1)
    augmented = jnp.where(lanes == rows + rank, 1.0, inner)
    blocks = [augmented[8 * i : 8 * i + 8, :] for i in range(rank // 8)]
    sub = lax.broadcasted_iota(jnp.int32, (8, wide), 0)

    def columns(block, p):
        return [jnp.broadcast_to(block[:, 8 * p + m : 8 * p + m + 1], (8, wide)) for m in range(8)]

    for p in range(rank // 8):
        panel, block = columns(blocks[p], p), blocks[p]
        pivot_rows, factors = [], []
        for j in range(8):
            inv = 1.0 / panel[j][j : j + 1, :]
            pivot_rows.append(block[j : j + 1, :] * inv)
            factors.append([panel[m][j : j + 1, :] * inv for m in range(j + 1, 8)])
            below = jnp.where(sub > j, panel[j], 0.0)
            block = block - below * pivot_rows[j]
            for m in range(j + 1, 8):
                panel[m] = panel[m] - below * factors[j][m - j - 1]
        blocks[p] = block
        for i in range(p + 1, rank // 8):
            panel, block = columns(blocks[i], p), blocks[i]
            for j in range(8):
                block = block - panel[j] * pivot_rows[j]
                for m in range(j + 1, 8):
                    panel[m] = panel[m] - panel[j] * factors[j][m - j - 1]
            blocks[i] = block
    reduced = jnp.concatenate(blocks, axis=0)
    pivots = jnp.sum(jnp.where(lanes == rows, reduced, 0.0), axis=1, keepdims=True)
    return reduced * (1.0 / jnp.sqrt(pivots))


def halves(value):
    high = value.astype(jnp.bfloat16)
    return high, (value - high.astype(jnp.float32)).astype(jnp.bfloat16)


def thirds(value):
    high, rest = value.astype(jnp.bfloat16), value
    rest = rest - high.astype(jnp.float32)
    middle = rest.astype(jnp.bfloat16)
    return high, middle, (rest - middle.astype(jnp.float32)).astype(jnp.bfloat16)


def kernel(nf, nz, field, start_hbm, out, start_t, fbuf, lbuf, fparts, lparts, cparts, part, extra, rbuf, zsrc, zbuf,
           gsrc, gbuf, osrc, lsrc, a_send, a_recv, own_sem, start_sem, l_send, l_recv, own_last, r_send, r_recv, z_send,
           z_recv, g_send, g_recv, o_send, o_recv, p_send, p_recv, plane_in, z_in):
    side = {16: 4, 4: 2}[nf]
    width_x = field.shape[2]
    rank, full_x = start_t.shape
    last = field.shape[0] - 1
    plane = nf * CORES
    f = lax.axis_index("fib")
    b = lax.axis_index("blk")
    core, z = lax.rem(b, CORES), lax.div(b, CORES)
    t = f * CORES + core
    row, col = lax.div(f, side), lax.rem(f, side)
    shift = lax.rem(b, 4)
    row_unit = row if side == 4 else f
    is_owner = owner_of(row_unit, shift, side) == f
    mine = pl.ds(pl.multiple_of(f * width_x, width_x), width_x)
    others = pl.ds(0, (nf - 1) * width_x)

    steps = [(dy, dx) for dy in range(side) for dx in range(side)]
    steps.sort(key=lambda s: -ring_distance(s[0], side) - ring_distance(s[1], side))
    row_at = [lax.rem(row + d, side) * side for d in range(side)]
    col_at = [lax.rem(col + d, side) for d in range(side)]
    fibs = [row_at[dy] + col_at[dx] for dy, dx in steps]
    fib_peers = fibs[:-1]
    twin = z * CORES + 1 - core
    plane_peers = []
    for other in fibs:
        if other is not fibs[-1]:
            plane_peers.append((other * CORES + core, {"fib": other, "blk": b}))
        plane_peers.append((other * CORES + 1 - core, {"fib": other, "blk": twin}))
    z_steps = sorted(range(1, nz), key=lambda k: -ring_distance(k, nz))
    z_peers = [{"fib": f, "blk": lax.rem(z + k, nz) * CORES + core} for k in z_steps]

    barrier = pltpu.get_barrier_semaphore()
    for other in fib_peers:
        pl.semaphore_signal(barrier, inc=1, device_id={"fib": other, "blk": z * CORES}, device_id_type=MESH)

    @pl.when(core == 1)
    def _():
        pl.semaphore_signal(barrier, inc=1, device_id={"fib": f, "blk": z * CORES}, device_id_type=MESH)

    for k in z_steps:
        device = {"fib": f, "blk": lax.rem(z + k, nz) * CORES + 1}
        pl.semaphore_signal(barrier, inc=1, device_id=device, device_id_type=MESH)
    pair = {"fib": f, "blk": twin}

    own = pltpu.make_async_copy(field.at[pl.ds(2 * f, 2)], fbuf.at[:, :, mine, :], own_sem)
    own.start()
    start_copy = pltpu.make_async_copy(start_hbm, start_t, start_sem)
    start_copy.start()

    @pl.when(core == 0)
    def _():
        pl.semaphore_wait(barrier, plane - 1)
        pl.semaphore_signal(plane_in, inc=1, device_id=pair, device_id_type=MESH)

    @pl.when(core == 1)
    def _():
        pl.semaphore_wait(plane_in, 1)

    def send_pair(q, _):
        s, zz = lax.div(q, 2), lax.rem(q, 2)
        for peer in fib_peers:
            pltpu.make_async_remote_copy(
                field.at[2 * peer + s, zz], fbuf.at[s, zz, mine, :], a_send, a_recv.at[q], {"fib": peer, "blk": b}, MESH
            ).start()
        return 0

    send_pair(0, 0)
    for u in range(4):
        owner = owner_of(u, shift, side)
        source = field.at[last, u // 2, :, pl.ds((u % 2) * 128, 128)]

        @pl.when(owner != f)
        def _():
            pltpu.make_async_remote_copy(source, lbuf.at[mine, :], l_send, l_recv, {"fib": owner, "blk": b}, MESH).start()

        @pl.when(owner == f)
        def _():
            pltpu.make_async_copy(source, lbuf.at[mine, :], own_last).start()

    lax.fori_loop(1, 3, send_pair, 0)
    for h in range(2):
        lanes = pl.ds(128 * h, 128)
        for peer in fib_peers:
            pltpu.make_async_remote_copy(
                field.at[2 * peer + 1, 1, :, lanes], fbuf.at[1, 1, mine, lanes], a_send, a_recv.at[3 + h],
                {"fib": peer, "blk": b}, MESH
            ).start()

    tiles_x = full_x // 128
    tiles = [(i, j) for i in range(rank // 8) for j in range(tiles_x)]

    def gram_term(fibres):
        projected = jnp.dot(start_t[...], fibres, precision=HIGHEST, preferred_element_type=jnp.float32)
        return lax.dot_general(projected, fibres, NT, precision=HIGHEST, preferred_element_type=jnp.float32)

    def times_halves(left, high, low, dims):
        left_high, left_low = halves(left)
        both = lax.dot_general(jnp.concatenate([left_high, left_low], axis=0), high, dims,
                               preferred_element_type=jnp.float32)
        return both[:rank] + both[rank:] + lax.dot_general(left_high, low, dims, preferred_element_type=jnp.float32)

    def gram_term_halves(fibres):
        high, low = halves(fibres)
        projected = times_halves(start_t[...], high, low, NN)
        return times_halves(projected, high, low, NT)

    extra[...] = jnp.zeros_like(extra)
    lparts[...] = jnp.zeros_like(lparts)
    cparts[...] = jnp.zeros_like(cparts)
    own.wait()
    start_copy.wait()
    chunks = [(0, 0, 0, 256), (0, 1, 0, 256), (1, 0, 0, 256), (1, 1, 0, 128), (1, 1, 128, 128)]
    raw_t = jnp.zeros((rank, full_x), jnp.float32)
    for q, (s, zz, first, width) in enumerate(chunks):
        whole = fbuf.at[s, zz, :, pl.ds(first, width)]
        pltpu.make_async_copy(whole.at[others, :], whole.at[others, :], a_recv.at[q]).wait()
        if q < 4:
            raw_t = raw_t + gram_term(whole[...])
        else:
            raw_t = gram_term_halves(whole[...])
        if q < 3:
            fparts[q, 0], fparts[q, 1], fparts[q, 2] = thirds(whole[...])
        if q == 1:
            @pl.when(is_owner)
            def _():
                pltpu.make_async_copy(lbuf.at[others, :], lbuf.at[others, :], l_recv).wait()
                pltpu.make_async_copy(lbuf.at[mine, :], lbuf.at[mine, :], own_last).wait()
                term = gram_term(lbuf[...])
                for n, (i, j) in enumerate(tiles):
                    extra[n] = term[8 * i : 8 * i + 8, 128 * j : 128 * j + 128]
                lparts[0], lparts[1], lparts[2] = thirds(lbuf[...])
        if q == 3:
            for n, (i, j) in enumerate(tiles):
                part[n] = raw_t[8 * i : 8 * i + 8, 128 * j : 128 * j + 128] + extra[n]
    for n, (i, j) in enumerate(tiles):
        part[n] += raw_t[8 * i : 8 * i + 8, 128 * j : 128 * j + 128]

    for other, device in plane_peers:
        pltpu.make_async_remote_copy(part.at[other], rbuf.at[t], r_send, r_recv, device, MESH).start()
    rbuf[t] = part[t]
    fparts[3, 0], fparts[3, 1], fparts[3, 2] = thirds(fbuf[1, 1])
    rest = pl.ds(0, plane - 1)

    @pl.when(core == 1)
    def _():
        pl.semaphore_wait(barrier, CORES * (nz - 1))
        pl.semaphore_signal(z_in, inc=1, device_id=pair, device_id_type=MESH)

    @pl.when(core == 0)
    def _():
        pl.semaphore_wait(z_in, 1)

    pltpu.make_async_copy(rbuf.at[rest], rbuf.at[rest], r_recv).wait()
    tile = jnp.sum(rbuf[...], axis=0)
    zsrc[...] = tile
    for device in z_peers:
        pltpu.make_async_remote_copy(zsrc, zbuf.at[z], z_send, z_recv, device, MESH).start()
    zbuf[z] = tile
    rest_z = pl.ds(0, nz - 1)
    pltpu.make_async_copy(zbuf.at[rest_z], zbuf.at[rest_z], z_recv).wait()
    tile = jnp.sum(zbuf[...], axis=0)
    gsrc[...] = tile
    for _, device in plane_peers:
        pltpu.make_async_remote_copy(gsrc, gbuf.at[t], g_send, g_recv, device, MESH).start()
    gbuf[t] = tile
    pltpu.make_async_copy(gbuf.at[rest], gbuf.at[rest], g_recv).wait()
    total_t = jnp.concatenate(
        [jnp.concatenate([gbuf[i * tiles_x + j] for j in range(tiles_x)], axis=1) for i in range(rank // 8)], axis=0)

    share = rank // nf
    high, middle, low = thirds(total_t)
    stack = jnp.concatenate([high, middle, low], axis=0)

    def products(parts, dims=NN, stack=stack):
        first = lax.dot_general(stack, parts[0], dims, preferred_element_type=jnp.float32)
        second = lax.dot_general(stack[: 2 * rank], parts[1], dims, preferred_element_type=jnp.float32)
        third = lax.dot_general(stack[:rank], parts[2], dims, preferred_element_type=jnp.float32)
        return first[:rank] + (second[:rank] + first[rank : 2 * rank]) + (
            third + second[rank:] + first[2 * rank :])

    padding = jnp.zeros((128 - rank, full_x), jnp.float32)
    zeros_right = padding.astype(jnp.bfloat16)
    wide = [jnp.concatenate([value, zeros_right], axis=0) for value in (high, middle, low)]
    inner = products(wide, NT)
    for q in range(4):
        cparts[:, rank : 2 * rank, 256 * q : 256 * q + 256] = jnp.stack(thirds(products(fparts[q])))
    cparts[:, rank : 2 * rank, 1024:] = jnp.stack(thirds(products(lparts[...])))
    inverse = jnp.concatenate(thirds(eliminate(inner, rank)), axis=0)

    def core_of(lanes):
        return products(cparts[:, :, lanes], NN, inverse)

    for q in range(4):
        core_part = core_of(pl.ds(256 * q, 256))
        for j in range(nf):
            osrc[j, q // 2, q % 2] = core_part[share * j : share * j + share, :]
    core_part = core_of(pl.ds(1024, 128))
    for j in range(nf):
        lsrc[j] = core_part[share * j : share * j + share, :]
    target = out.at[pl.ds(2 * f, 2)]
    last_lanes = pl.ds(pl.multiple_of(lax.rem(row_unit, 2) * 128, 128), 128)
    last_target = out.at[last, lax.div(row_unit, 2), :, last_lanes]
    def send_core(with_last):
        for peer in fib_peers:
            device = {"fib": peer, "blk": b}
            pltpu.make_async_remote_copy(osrc.at[peer], target, o_send, o_recv, device, MESH).start()
            if with_last:
                pltpu.make_async_remote_copy(lsrc.at[peer], last_target, p_send, p_recv, device, MESH).start()

    @pl.when(is_owner)
    def _():
        send_core(True)

    @pl.when(jnp.logical_not(is_owner))
    def _():
        send_core(False)

    own_core = pltpu.make_async_copy(osrc.at[f], target, own_sem)
    own_core.start()

    @pl.when(is_owner)
    def _():
        own_unit = pltpu.make_async_copy(lsrc.at[f], last_target, own_last)
        own_unit.start()
        own_unit.wait()

    sent = fbuf.at[:, :, others, :]
    pltpu.make_async_copy(sent, sent, a_send).wait()
    pltpu.make_async_copy(rbuf.at[rest], rbuf.at[rest], r_send).wait()
    pltpu.make_async_copy(zbuf.at[rest_z], zbuf.at[rest_z], z_send).wait()
    pltpu.make_async_copy(gbuf.at[rest], gbuf.at[rest], g_send).wait()
    own_core.wait()
    arrived = out.at[pl.ds(0, 2 * (nf - 1))]
    pltpu.make_async_copy(arrived, arrived, o_send).wait()
    pltpu.make_async_copy(arrived, arrived, o_recv).wait()

    def finish_last(units):
        slab = lbuf.at[pl.ds(0, units * width_x), :]
        pltpu.make_async_copy(slab, slab, l_send).wait()
        pltpu.make_async_copy(lsrc.at[pl.ds(0, units)], lsrc.at[pl.ds(0, units)], p_recv).wait()

    @pl.when(is_owner)
    def _():
        finish_last(3)
        pltpu.make_async_copy(lsrc.at[pl.ds(0, nf - 1)], lsrc.at[pl.ds(0, nf - 1)], p_send).wait()

    if side == 4:
        @pl.when(jnp.logical_not(is_owner))
        def _():
            finish_last(4)


def solution(mesh):
    nf, nb = mesh.shape["fib"], mesh.shape["blk"]
    nz = nb // CORES

    def shards(field_data, start_block):
        species, planes, width_x, width_y = field_data.shape
        full_x, rank = start_block.shape
        share = rank // nf
        tiles = rank * full_x // 1024
        assert species == 2 * nf + 1 and planes == 2 and width_y == 256 and tiles == nf * CORES and 2 * rank <= 128
        f32, bf16 = jnp.float32, jnp.bfloat16
        dma = pltpu.SemaphoreType.DMA
        return pl.pallas_call(
            functools.partial(kernel, nf, nz),
            out_shape=jax.ShapeDtypeStruct((species, planes, share, width_y), f32),
            in_specs=[pl.BlockSpec(memory_space=pltpu.HBM), pl.BlockSpec(memory_space=pltpu.HBM)],
            out_specs=pl.BlockSpec(memory_space=pl.ANY),
            scratch_shapes=[
                pltpu.VMEM((rank, full_x), f32),
                pltpu.VMEM((2, 2, full_x, width_y), f32),
                pltpu.VMEM((full_x, 128), f32),
                pltpu.VMEM((4, 3, full_x, width_y), bf16),
                pltpu.VMEM((3, full_x, 128), bf16),
                pltpu.VMEM((3, 128, 4 * width_y + 128), bf16),
                pltpu.VMEM((tiles, 8, 128), f32),
                pltpu.VMEM((tiles, 8, 128), f32),
                pltpu.VMEM((tiles, 8, 128), f32),
                pltpu.VMEM((8, 128), f32),
                pltpu.VMEM((nz, 8, 128), f32),
                pltpu.VMEM((8, 128), f32),
                pltpu.VMEM((tiles, 8, 128), f32),
                pltpu.VMEM((nf, 2, 2, share, width_y), f32),
                pltpu.VMEM((nf, share, 128), f32),
                dma, dma((5,)), dma, dma, dma, dma, dma, dma, dma, dma, dma, dma, dma, dma, dma, dma, dma,
                pltpu.SemaphoreType.REGULAR, pltpu.SemaphoreType.REGULAR,
            ],
            compiler_params=pltpu.CompilerParams(collective_id=0, has_side_effects=True, vmem_limit_bytes=48 << 20),
            cost_estimate=pl.CostEstimate(flops=2_000_000_000, bytes_accessed=5_000_000, transcendentals=64),
            name="hosvd_step",
        )(pltpu.with_memory_space_constraint(field_data, pltpu.HBM), pltpu.with_memory_space_constraint(start_block.T, pltpu.HBM))

    in_specs = (P(None, "blk", "fib", None), P())
    out_specs = P(None, "blk", "fib", None)
    return jax.shard_map(shards, mesh=mesh, in_specs=in_specs, out_specs=out_specs, check_vma=False)
```
